512 devices in a mesh: gx: 16 (over z_lo, core), gy: 32 (over x, z_hi, y).
Axes of the slice: x: 4, y: 4, z: 16 (z_hi: 2, z_lo: 8; z = z_hi * 8 + z_lo), core: 2. Of those that a mesh axis runs over, the one named last changes fastest.
Arguments:
- positions: float32 [3, 16, 32, 128], P(None, 'gx', 'gy'), may hold values from 0 to 20
- spring: float32 [16, 32, 128], P('gx', 'gy'), may hold values from 0.25 to 4
- border: int32 [16, 32, 32], P('gx', 'gy'), may hold values from 0 to 127, as said below
- neighbours: int32 [16, 32, 64, 128], P('gx', 'gy'), may hold values from -1 to 1055, as said below
- vec_prev: float32 [3, 8, 16, 32, 128], P(None, None, 'gx', 'gy'), may hold values from -6 to 6
- vec_now: float32 [3, 8, 16, 32, 128], P(None, None, 'gx', 'gy'), may hold values from -6 to 6
- heat_prev: float32 [3, 8, 16, 32, 128], P(None, None, 'gx', 'gy'), may hold values from -6 to 6
- heat_now: float32 [3, 8, 16, 32, 128], P(None, None, 'gx', 'gy'), may hold values from -6 to 6
Outputs:
- vec_next: float32 [3, 8, 16, 32, 128], P(None, None, 'gx', 'gy')
- vec_after: float32 [3, 8, 16, 32, 128], P(None, None, 'gx', 'gy')
- heat_next: float32 [3, 8, 16, 32, 128], P(None, None, 'gx', 'gy')
- heat_after: float32 [3, 8, 16, 32, 128], P(None, None, 'gx', 'gy')
The draws below stay inside these ranges and needn't reach their ends.
Inputs may be any that keep to these rules, and one draw needn't show every extreme that they name: `border`: each column's row lists 32 different atoms of that column. `neighbours`: -1 marks an empty slot, and empty slots follow the used ones; an entry o * 128 + k names for o = 4 the column's own atom k, else entry k (k < 32) of the border table of the column o // 3 - 1 steps along x and o % 3 - 1 steps along y (periodic); every atom uses at least 32 slots and some atom of every column uses all 64.
All inputs are finite; a program needn't handle non-finite values.
Results may differ from the reference program's by a relative error of at most 0.0003.
Values sent between devices are 32-bit elements; how exact they have to be, the bound alone decides.
No kernel may reach another device: no remote copies, remote signals or barrier semaphores. Data moves between devices by JAX's collectives and lax.ppermute only.
A program may use at most 64 MiB of HBM per device.

```python
import math
import jax
import jax.numpy as jnp
from jax import lax

A = 128
R = 8
NB = 64
G = 32
COLS_X = 16
COLS_Y = 32


def draw_border(key, part):
    keys = jax.random.split(jax.random.fold_in(key, 5), COLS_X * COLS_Y)
    chosen_rows = jax.vmap(lambda k: jax.random.permutation(k, A)[:G])(keys)
    return chosen_rows.reshape(COLS_X, COLS_Y, G).astype(jnp.int32)


def draw_neighbours(key, part):
    keys = jax.random.split(jax.random.fold_in(key, 11), 5)
    shape = (COLS_X, COLS_Y, NB, A)
    picked = jax.random.randint(keys[0], shape, 0, 16)
    offset = jnp.where(picked >= 9, 4, picked)
    own_atom = jax.random.randint(keys[1], shape, 0, A)
    border_slot = jax.random.randint(keys[2], shape, 0, G)
    within = jnp.where(offset == 4, own_atom, border_slot)
    counts = jax.random.randint(keys[3], (COLS_X, COLS_Y, 1, A), NB // 2, NB + 1)
    fullest = jax.random.randint(keys[4], (COLS_X, COLS_Y, 1, 1), 0, A)
    counts = jnp.where(jnp.arange(A)[None, None, None, :] == fullest, NB, counts)
    live = jnp.arange(NB)[None, None, :, None] < counts
    return jnp.where(live, offset * A + within, -1).astype(jnp.int32)


def shard_levels(rng, extent, pieces, low, largest):
    def one(dim, parts):
        heights = jax.random.uniform(jax.random.fold_in(jax.random.fold_in(rng, 6), dim), (parts,), jnp.float32, low / len(pieces), largest / len(pieces))
        return jnp.repeat(jnp.exp(heights), extent[dim] // parts).reshape((-1,) + (1,) * (len(extent) - dim - 1))

    factor_of = one(*pieces[0])
    for cut in pieces[1:]:
        factor_of = factor_of * one(*cut)
    return factor_of


def noise(rng, extent, deviation, reach, cuts=(), kind=jnp.bfloat16):
    loudness = shard_levels(rng, extent, cuts, -0.22, 0.18) if cuts else 1.0
    values = jax.random.normal(rng, extent, jnp.float32) * deviation * loudness
    return jnp.minimum(jnp.maximum(values, -reach), reach).astype(kind)


def setup_inputs(seed: int = 0) -> dict:
    arg_keys = jax.random.split(jax.random.key(seed), 9)
    positions = jnp.clip(20.0 * jax.random.uniform(arg_keys[0], (3, COLS_X, COLS_Y, A), jnp.float32) ** shard_levels(arg_keys[0], (3, COLS_X, COLS_Y, A), ((1, 16), (2, 32)), -0.2, 0.2), 0.0, 20.0)
    spring = jnp.clip(jnp.exp(math.log(4.0) - 2.7725887 * jax.random.uniform(arg_keys[1], (COLS_X, COLS_Y, A), jnp.float32) ** shard_levels(arg_keys[1], (COLS_X, COLS_Y, A), ((0, 16), (1, 32)), -0.2, 0.2)), 0.25, 4.0)
    border = draw_border(jax.random.fold_in(arg_keys[8], 71), 0)
    neighbours = draw_neighbours(jax.random.fold_in(arg_keys[8], 71), 0)
    vec_prev = noise(arg_keys[4], (3, R, COLS_X, COLS_Y, A), 1.0, 6.0, ((2, 16), (3, 32)), jnp.float32)
    vec_now = noise(arg_keys[5], (3, R, COLS_X, COLS_Y, A), 1.0, 6.0, ((2, 16), (3, 32)), jnp.float32)
    heat_prev = noise(arg_keys[6], (3, R, COLS_X, COLS_Y, A), 1.0, 6.0, ((2, 16), (3, 32)), jnp.float32)
    heat_now = noise(arg_keys[7], (3, R, COLS_X, COLS_Y, A), 1.0, 6.0, ((2, 16), (3, 32)), jnp.float32)
    return dict(positions=positions, spring=spring, border=border, neighbours=neighbours, vec_prev=vec_prev, vec_now=vec_now, heat_prev=heat_prev, heat_now=heat_now)


column_edge = 20.0
reach_sq = 64.0

def reference(positions, spring, border, neighbours, vec_prev, vec_now, heat_prev, heat_now):
    cols_x, cols_y, n_atoms = spring.shape
    n_slots = neighbours.shape[2]
    n_border = border.shape[-1]
    n_vec = vec_prev.shape[1]
    flat_pos = positions.reshape(3, -1)
    flat_spring = spring.reshape(-1)
    flat_border = border.reshape(-1)
    grid_x = jnp.arange(cols_x, dtype=jnp.int32)[:, None, None]
    grid_y = jnp.arange(cols_y, dtype=jnp.int32)[None, :, None]
    slot_major = jnp.moveaxis(neighbours, 2, 0)

    def operate_on(current):
        n_rows = current.shape[1]
        flat_cur = current.reshape(3, n_rows, -1)

        def slot_step(total, entries):
            usable = entries >= 0
            entry_safe = jnp.maximum(entries, 0)
            offset = entry_safe // n_atoms
            within = entry_safe % n_atoms
            step_x = offset // 3 - 1
            step_y = offset % 3 - 1
            column = (grid_x + step_x) % cols_x * cols_y + (grid_y + step_y) % cols_y
            lookup = jnp.take(flat_border, column * n_border + jnp.minimum(within, n_border - 1))
            atom = jnp.where(offset == 4, within, lookup)
            flat = (column * n_atoms + atom).reshape(-1).astype(jnp.int32)
            far_pos = flat_pos[:, flat].reshape(3, cols_x, cols_y, n_atoms)
            far_spring = flat_spring[flat].reshape(cols_x, cols_y, n_atoms)
            delta_x = far_pos[0] + step_x.astype(jnp.float32) * column_edge - positions[0]
            delta_y = far_pos[1] + step_y.astype(jnp.float32) * column_edge - positions[1]
            delta_z = far_pos[2] - positions[2]
            dist_sq = delta_x * delta_x + delta_y * delta_y + delta_z * delta_z
            coupling = jnp.where(usable, jnp.sqrt(spring * far_spring) / (n_slots * (1.0 + dist_sq / reach_sq)), jnp.float32(0.0))
            bending = 2.0 / (dist_sq + 1.0)
            far_rows = flat_cur[:, :, flat].reshape(3, n_rows, cols_x, cols_y, n_atoms)
            u = current - far_rows
            proj = delta_x * u[0] + delta_y * u[1] + delta_z * u[2]
            displace = jnp.stack([delta_x, delta_y, delta_z])[:, None]
            contrib = coupling * (u + bending * displace * proj[None])
            return (total + contrib, None)
        total, _ = lax.scan(slot_step, jnp.zeros_like(current), slot_major)
        return total - current
    state_zero = jnp.concatenate([vec_prev, heat_prev], axis=1)
    state_one = jnp.concatenate([vec_now, heat_now], axis=1)
    state_two = 2.0 * operate_on(state_one) - state_zero
    state_three = 2.0 * operate_on(state_two) - state_one
    return (state_two[:, :n_vec], state_three[:, :n_vec], state_two[:, n_vec:], state_three[:, n_vec:])
```

```python
import jax
import jax.numpy as jnp
from jax import lax
from jax.experimental import pallas as pl
from jax.experimental.pallas import tpu as pltpu
from jax.sharding import PartitionSpec as P

column_edge = 20.0
reach_sq = 64.0
A = 128
G = 32
NB = 64
F = 16
OWN = 3 * A
FAR = 8 * A
F32 = jnp.float32
BF16 = jnp.bfloat16
KEYS = ((0, 0), (0, 1), (0, 2), (1, 1), (1, 2), (2, 2))


def steps_of_slots():
    e = 1 - 2 * lax.rem(lax.axis_index("gy"), 2)
    f = 1 - 2 * lax.rem(lax.axis_index("gx"), 2)
    return [(0, e), (0, -e)] + [(s, t) for s in (f, -f) for t in (e, 0, -e)]


def gather_slots(near, row_one, row_two):
    return [near[0][...], near[1][...]] + [r[j] for r in (row_one, row_two) for j in range(3)]


def split(x):
    high = x.astype(BF16)
    return high, (x - high.astype(F32)).astype(BF16)


def border_lanes(border, values):
    index = jnp.concatenate([border[...]] * (A // G), axis=1)
    return jnp.take_along_axis(values, jnp.broadcast_to(index, values.shape), axis=1)


def pack_fields(border, parts, last):
    group = lax.broadcasted_iota(jnp.int32, (F, A), 1) // G
    out = last
    for b in range(3):
        out = jnp.where(group == b, border_lanes(border, parts[b]), out)
    return out


def stacked(vec, heat):
    return [jnp.concatenate([vec[b], heat[b]], axis=0) for b in range(3)]


def pack_kernel(pos, spring, border, vec, heat, out):
    geometry = jnp.concatenate(
        [pos[0], pos[1], pos[2], spring[...], jnp.zeros((F - 4, A), F32)], axis=0
    )
    out[...] = pack_fields(border, stacked(vec, heat), border_lanes(border, geometry))


def count_slots(entries, groups):
    sub = lax.broadcasted_iota(jnp.int32, (8, A), 0)
    counters = [jnp.zeros((8, A), jnp.int32) for _ in groups]
    for n in range(NB):
        e = jnp.broadcast_to(entries[n : n + 1, :], (8, A))
        mark = jnp.where(sub == (e & 7), jnp.left_shift(jnp.int32(1), e & 24), 0)
        which = lax.shift_right_arithmetic(e, 5)
        for i, g in enumerate(groups):
            counters[i] += jnp.where(which == g, mark, 0)
    return counters


def pair_terms(counter, source, home, root_home):
    tiles = [lax.shift_right_logical(counter, 8 * q) & 255 for q in range(4)]
    count = jnp.concatenate(tiles, axis=0).astype(F32)
    d = [source[a] - home[a] for a in range(3)]
    r2 = d[0] * d[0] + d[1] * d[1] + d[2] * d[2]
    near = r2 + 1.0
    inverse = (count * (root_home * source[3])) / ((reach_sq + r2) * near)
    c = inverse * near * (reach_sq / NB)
    bend = inverse * (2.0 * reach_sq / NB)
    g = [bend * d[a] for a in range(3)]
    return {(a, b): (g[a] * d[b] + c if a == b else g[a] * d[b]) for a, b in KEYS}


def put_terms(w_high, w_low, sums, rows, terms):
    for (a, b), value in terms.items():
        part = value[0:8] + value[8:16] + value[16:24] + value[24:32]
        sums[(a, b)] = sums[(a, b)] + part if (a, b) in sums else part
        high, low = split(value)
        for p, q in sorted({(a, b), (b, a)}):
            w_high[rows[q] : rows[q] + G, p * A : (p + 1) * A] = high
            w_low[rows[q] : rows[q] + G, p * A : (p + 1) * A] = low


def apply_weights(w_high, w_low, lhs):
    high, low = split(lhs)
    both = jnp.concatenate([high, low], axis=0)
    main = jnp.dot(both, w_high[...], preferred_element_type=F32)
    rest = jnp.dot(high, w_low[...], preferred_element_type=F32)
    return main[:F] + main[F:] + rest


def home_of(pos, root):
    home = [jnp.broadcast_to(pos[a], (G, A)) for a in range(3)]
    return home, jnp.broadcast_to(root, (G, A))


def own_kernel(pos, spring, entries, vec, heat, w_high, w_low, far, counts, sums_out):
    groups = [4 * (3 * (sx + 1) + sy + 1) for sx, sy in steps_of_slots()]
    counters = count_slots(entries[...], groups + [16, 17, 18, 19])
    for i in range(8):
        counts[i] = counters[i]
    root = jnp.sqrt(spring[...])
    home, root_home = home_of(pos, root)
    geo = jnp.concatenate([pos[0], pos[1], pos[2], root, jnp.zeros((4, A), F32)], axis=0).T
    sums = {}
    for t in range(4):
        source = [
            jnp.broadcast_to(geo[t * G : (t + 1) * G, c : c + 1], (G, A)) for c in range(4)
        ]
        terms = pair_terms(counters[8 + t], source, home, root_home)
        put_terms(w_high, w_low, sums, [b * A + t * G for b in range(3)], terms)
    for i, key in enumerate(KEYS):
        sums_out[i] = sums[key]
    far[...] = apply_weights(w_high, w_low, jnp.concatenate(stacked(vec, heat), axis=1))


def local_term(far, self_terms, current, previous, a):
    total = -far[:, a * A : (a + 1) * A] - current[a]
    for b in range(3):
        total += self_terms[(min(a, b), max(a, b))] * current[b]
    return 2.0 * total - previous[a]


def first_kernel(pos, spring, border, vec, heat, vec0, heat0, far_in, counts, sums_in,
                 near_one, near_two, row_one, row_two,
                 next_v, next_h, payload, w_high, w_low, self_out):
    slots = gather_slots((near_one, near_two), row_one, row_two)
    root = jnp.sqrt(spring[...])
    home, root_home = home_of(pos, root)
    geo = jnp.concatenate([s[0:4] for s in slots], axis=0).T
    sums = {key: sums_in[i] for i, key in enumerate(KEYS)}
    for j, (sx, sy) in enumerate(steps_of_slots()):
        cols = [geo[3 * G :, 4 * j + c : 4 * j + c + 1] for c in range(4)]
        source = [
            jnp.broadcast_to(cols[0] + column_edge * jnp.asarray(sx, F32), (G, A)),
            jnp.broadcast_to(cols[1] + column_edge * jnp.asarray(sy, F32), (G, A)),
            jnp.broadcast_to(cols[2], (G, A)),
            jnp.broadcast_to(jnp.sqrt(cols[3]), (G, A)),
        ]
        terms = pair_terms(counts[j], source, home, root_home)
        put_terms(w_high, w_low, sums, [j * A + b * G for b in range(3)], terms)
        w_high[j * A + 3 * G : (j + 1) * A, :] = jnp.zeros((G, OWN), BF16)
        w_low[j * A + 3 * G : (j + 1) * A, :] = jnp.zeros((G, OWN), BF16)
    self_terms = {}
    for i, key in enumerate(KEYS):
        self_terms[key] = jnp.sum(sums[key], axis=0, keepdims=True)
        self_out[i : i + 1, :] = self_terms[key]
    far = far_in[...] + apply_weights(w_high, w_low, jnp.concatenate(slots, axis=1))
    current, previous = stacked(vec, heat), stacked(vec0, heat0)
    result = [local_term(far, self_terms, current, previous, a) for a in range(3)]
    payload[...] = pack_fields(border, result, jnp.zeros((F, A), F32))
    for a in range(3):
        next_v[a] = result[a][:8]
        next_h[a] = result[a][8:]


def again_kernel(w_high, w_low, self_in, vec, heat, vec1, heat1, out):
    self_terms = {key: self_in[i : i + 1, :] for i, key in enumerate(KEYS)}
    current, previous = stacked(vec, heat), stacked(vec1, heat1)
    far = apply_weights(w_high, w_low, jnp.concatenate(current, axis=1))
    for a in range(3):
        out[a] = local_term(far, self_terms, current, previous, a)


def last_kernel(w_high, w_low, partial, near_one, near_two, row_one, row_two, out_v, out_h):
    slots = gather_slots((near_one, near_two), row_one, row_two)
    far = apply_weights(w_high, w_low, jnp.concatenate(slots, axis=1))
    for a in range(3):
        result = partial[a] - 2.0 * far[:, a * A : (a + 1) * A]
        out_v[a] = result[:8]
        out_h[a] = result[8:]


def pairs(count, first):
    out = []
    for i in range(first, count + first, 2):
        a, b = i % count, (i + 1) % count
        out += [(a, b), (b, a)]
    return out


def swaps(values, axis):
    count = lax.axis_size(axis)
    return [lax.ppermute(values, axis, pairs(count, first)) for first in (0, 1)]


def surround(payload):
    near_one, near_two = swaps(payload, "gy")
    row_one, row_two = swaps(jnp.stack([near_one, payload, near_two]), "gx")
    return near_one, near_two, row_one, row_two


def call(kernel, out_shape, *args):
    size = sum(x.size * x.dtype.itemsize for x in (*args, *out_shape))
    return pl.pallas_call(
        kernel,
        out_shape=out_shape,
        name=kernel.__name__,
        cost_estimate=pl.CostEstimate(flops=2**20, bytes_accessed=size, transcendentals=0),
        compiler_params=pltpu.CompilerParams(vmem_limit_bytes=16 * 2**20),
    )(*args)


def shards(positions, spring, border, neighbours, vec_prev, vec_now, heat_prev, heat_now):
    def fields(x):
        return x.reshape(3, 8, A)

    shape = jax.ShapeDtypeStruct
    vector = shape((3, 8, A), F32)
    pos = positions.reshape(3, 1, A)
    stiff = spring.reshape(1, A)
    index = border.reshape(1, G)
    entries = neighbours.reshape(NB, A)
    v0, v1, h0, h1 = map(fields, (vec_prev, vec_now, heat_prev, heat_now))
    (payload,) = call(pack_kernel, (shape((F, A), F32),), pos, stiff, index, v1, h1)
    received = surround(payload)
    own_high, own_low, far, counts, sums = call(
        own_kernel,
        (
            shape((OWN, OWN), BF16),
            shape((OWN, OWN), BF16),
            shape((F, OWN), F32),
            shape((8, 8, A), jnp.int32),
            shape((6, 8, A), F32),
        ),
        pos, stiff, entries, v1, h1,
    )
    v2, h2, payload, far_high, far_low, self_terms = call(
        first_kernel,
        (
            vector,
            vector,
            shape((F, A), F32),
            shape((FAR, OWN), BF16),
            shape((FAR, OWN), BF16),
            shape((6, A), F32),
        ),
        pos, stiff, index, v1, h1, v0, h0, far, counts, sums, *received,
    )
    received = surround(payload)
    (partial,) = call(
        again_kernel, (shape((3, F, A), F32),), own_high, own_low, self_terms, v2, h2, v1, h1
    )
    v3, h3 = call(last_kernel, (vector, vector), far_high, far_low, partial, *received)
    whole = vec_prev.shape
    return v2.reshape(whole), v3.reshape(whole), h2.reshape(whole), h3.reshape(whole)


def solution(mesh):
    wide = P(None, None, "gx", "gy", None)
    return jax.shard_map(
        shards,
        mesh=mesh,
        in_specs=(
            P(None, "gx", "gy", None),
            P("gx", "gy", None),
            P("gx", "gy", None),
            P("gx", "gy", None, None),
            wide, wide, wide, wide,
        ),
        out_specs=(wide, wide, wide, wide),
        check_vma=False,
    )
```

```python
import functools

import jax
import jax.numpy as jnp
from jax import lax
from jax.experimental import pallas as pl
from jax.experimental.pallas import tpu as pltpu
from jax.sharding import PartitionSpec as P

column_edge = 20.0
reach_sq = 64.0
A = 128
G = 32
NB = 64
F = 16
OWN = 3 * A
F32 = jnp.float32
BF16 = jnp.bfloat16
KEYS = ((0, 0), (0, 1), (0, 2), (1, 1), (1, 2), (2, 2))
RING = ((-1, -1), (-1, 0), (-1, 1), (0, -1), (0, 1), (1, -1), (1, 0), (1, 1))
WIDE = tuple((x, y) for x in range(-2, 3) for y in range(-2, 3))
KINDS = 3


def other(i, count):
    return (i + 1) % count if i % 2 else (i - 1) % count


def routes(nx, ny):
    def pair_x(x, y):
        return x ^ 1, y

    def pair_y(x, y):
        return x, y ^ 1

    def across_y(x, y):
        return (x, other(y, ny)) if y % 4 in (0, 3) else None

    def across_x(x, y):
        return (other(x, nx), y) if y % 4 in (1, 2) else None

    def beside(x, y):
        if y % 4 in (1, 2):
            return x, other(y, ny)
        if x in (0, nx - 1):
            return other(x, nx), other(y, ny)
        return other(x, nx), y

    return (
        (pair_y, -1),
        (pair_x, 0),
        (across_x, 1),
        (across_y, 0),
        (pair_x, 3),
        (beside, 4),
        (pair_x, 5),
        (pair_y, 6),
    )


def class_of(x, y, nx):
    return 4 * (0 if x == 0 else 3 if x == nx - 1 else 1 + (x + 1) % 2) + y % 4


@functools.lru_cache(None)
def make_plan(nx, ny):
    devices = [(x, y) for x in range(nx) for y in range(ny)]
    steps = routes(nx, ny)

    def wanted(x, y):
        return [
            (kind, (x + a) % nx, (y + b) % ny)
            for kind in range(KINDS)
            for a, b in (WIDE if kind == 0 else RING)
        ]

    known = [{d: {(k, *d) for k in range(KINDS)} for d in devices}]
    for target, base in steps:
        later = {d: set(known[-1][d]) for d in devices}
        for d in devices:
            if target(*d):
                later[target(*d)] |= known[base + 1][d]
        known.append(later)
    first = {d: {} for d in devices}
    for t, state in enumerate(known):
        for d in devices:
            for item in state[d]:
                first[d].setdefault(item, t)
    demand = {d: set(wanted(*d)) for d in devices}
    assert all(demand[d] <= known[-1][d] for d in devices)
    sent = [None] * len(steps)
    for i in reversed(range(len(steps))):
        target, base = steps[i]
        sent[i] = {}
        for d in devices:
            t = target(*d)
            if t is None:
                sent[i][d] = []
                continue
            items = {m for m in demand[t] if first[t][m] == i + 1 and m in known[base + 1][d]}
            near = lambda v, count: (v + count // 2) % count
            sent[i][d] = sorted(
                items, key=lambda m: (m[0], near(m[1] - t[0], nx), near(m[2] - t[1], ny))
            )
        for d in devices:
            demand[d] |= set(sent[i][d])
    sizes = [max(1, *(len(v) for v in s.values())) for s in sent]
    starts = [KINDS + sum(sizes[:i]) for i in range(len(sizes))]
    place = {d: {(k, *d): k for k in range(KINDS)} for d in devices}
    for i, (target, _) in enumerate(steps):
        for d in devices:
            for j, item in enumerate(sent[i][d]):
                place[target(*d)].setdefault(item, starts[i] + j)
    send_rows = [{} for _ in steps]
    last_rows = {}
    for d in devices:
        c = class_of(*d, nx)
        for i in range(len(steps)):
            row = tuple(place[d][item] for item in sent[i][d])
            assert send_rows[i].setdefault(c, row) == row
        row = tuple(place[d][item] for item in wanted(*d))
        assert last_rows.setdefault(c, row) == row
    links = [
        [(x * ny + y, t[0] * ny + t[1]) for x, y in devices for t in [f(x, y)] if t]
        for f, _ in steps
    ]
    return steps, sizes, starts, send_rows, last_rows, links


def for_each_row(rows, nx, body):
    x, y = lax.axis_index("gx"), lax.axis_index("gy")
    column = jnp.where(x == 0, 0, jnp.where(x == nx - 1, 3, 1 + lax.rem(x + 1, 2)))
    mine = 4 * column + lax.rem(y, 4)
    classes = {}
    for c, row in rows.items():
        classes.setdefault(row, []).append(c)
    for row, members in classes.items():
        hit = mine == members[0]
        for c in members[1:]:
            hit = hit | (mine == c)
        pl.when(hit)(functools.partial(body, row))


def block_at(refs, starts, place):
    if place < KINDS:
        return refs[0][place]
    i = max(j for j in range(len(starts)) if starts[j] <= place)
    return refs[i + 1][place - starts[i]]


def relay_kernel(rows, starts, nx, *refs):
    out = refs[-1]

    def body(row):
        for j, place in enumerate(row):
            out[j] = block_at(refs, starts, place)
        for j in range(len(row), out.shape[0]):
            out[j] = jnp.zeros((F, A), F32)

    for_each_row(rows, nx, body)


def split(x):
    high = x.astype(BF16)
    return high, (x - high.astype(F32)).astype(BF16)


def border_lanes(border, values):
    index = jnp.concatenate([border[...]] * (A // G), axis=1)
    return jnp.take_along_axis(values, jnp.broadcast_to(index, values.shape), axis=1)


def by_group(parts):
    group = lax.broadcasted_iota(jnp.int32, parts[0].shape, 1) // G
    out = parts[3]
    for q in range(3):
        out = jnp.where(group == q, parts[q], out)
    return out


def stacked(vec, heat):
    return [jnp.concatenate([vec[b], heat[b]], axis=0) for b in range(3)]


def count_slots(entries, groups):
    sub = lax.broadcasted_iota(jnp.int32, (8, A), 0)
    counters = [jnp.zeros((8, A), jnp.int32) for _ in groups]
    for n in range(NB):
        e = jnp.broadcast_to(entries[n : n + 1, :], (8, A))
        mark = jnp.where(sub == (e & 7), jnp.left_shift(jnp.int32(1), e & 24), 0)
        which = lax.shift_right_arithmetic(e, 5)
        for i, g in enumerate(groups):
            counters[i] += jnp.where(which == g, mark, 0)
    return counters


FAR_GROUPS = [4 * (3 * (x + 1) + y + 1) for x, y in RING]


def pair_terms(counter, source, home):
    tiles = [lax.shift_right_logical(counter, 8 * q) & 255 for q in range(4)]
    count = jnp.concatenate(tiles, axis=0).astype(F32)
    d = [source[a] - home[a] for a in range(3)]
    r2 = d[0] * d[0] + d[1] * d[1] + d[2] * d[2]
    near = r2 + 1.0
    inverse = (count * (home[3] * source[3])) / ((reach_sq + r2) * near)
    c = inverse * near * (reach_sq / NB)
    bend = inverse * (2.0 * reach_sq / NB)
    g = [bend * d[a] for a in range(3)]
    return {(a, b): (g[a] * d[b] + c if a == b else g[a] * d[b]) for a, b in KEYS}


def put_terms(w_high, w_low, sums, rows, terms):
    for (a, b), value in terms.items():
        part = value[0:8] + value[8:16] + value[16:24] + value[24:32]
        sums[(a, b)] = sums[(a, b)] + part if (a, b) in sums else part
        high, low = split(value)
        for p, q in sorted({(a, b), (b, a)}):
            w_high[rows[q] : rows[q] + G, p * A : (p + 1) * A] = high
            w_low[rows[q] : rows[q] + G, p * A : (p + 1) * A] = low


def total(sums):
    return {key: jnp.sum(value, axis=0, keepdims=True) for key, value in sums.items()}


def apply_weights(w_high, w_low, lhs):
    high, low = split(lhs)
    both = jnp.concatenate([high, low], axis=0)
    main = jnp.dot(both, w_high[...], preferred_element_type=F32)
    rest = jnp.dot(high, w_low[...], preferred_element_type=F32)
    return main[:F] + main[F:] + rest


def self_product(terms, fields, a):
    return sum(terms[(min(a, b), max(a, b))] * fields[b] for b in range(3))


def spread(rows):
    return [jnp.broadcast_to(r, (G, A)) for r in rows]


def own_kernel(pos, spring, border, entries, vec, heat, vec0, heat0,
               payload, w_high, w_low, partial, self_out, counts):
    counters = count_slots(entries[...], FAR_GROUPS + [16, 17, 18, 19])
    for i in range(8):
        counts[i] = counters[i]
    root = jnp.sqrt(spring[...])
    home = spread([pos[0], pos[1], pos[2], root])
    geo = jnp.concatenate([pos[0], pos[1], pos[2], root, jnp.zeros((4, A), F32)], axis=0).T
    sums = {}
    for t in range(4):
        source = spread([geo[t * G : (t + 1) * G, c : c + 1] for c in range(4)])
        terms = pair_terms(counters[8 + t], source, home)
        put_terms(w_high, w_low, sums, [b * A + t * G for b in range(3)], terms)
    own_terms = total(sums)
    for i, key in enumerate(KEYS):
        self_out[i : i + 1, :] = own_terms[key]
    current, previous = stacked(vec, heat), stacked(vec0, heat0)
    far = apply_weights(w_high, w_low, jnp.concatenate(current, axis=1))
    begun = []
    for a in range(3):
        inner = self_product(own_terms, current, a) - far[:, a * A : (a + 1) * A] - current[a]
        begun.append(2.0 * inner - previous[a])
        partial[a] = begun[a]
    geometry = jnp.concatenate(
        [pos[0], pos[1], pos[2], spring[...], jnp.zeros((F - 4, A), F32)], axis=0
    )
    picked = functools.partial(border_lanes, border)
    lists = [picked(entries[F * s : F * (s + 1), :].astype(F32)) for s in range(4)]
    payload[0] = by_group([picked(x) for x in (*current, geometry)])
    payload[1] = by_group([picked(x) for x in begun] + [lists[3]])
    payload[2] = by_group(lists[:3] + [jnp.zeros((F, A), F32)])


def moved(block, source, target):
    shift = (target - source) % 4 * G
    return pltpu.roll(block, shift, 1) if shift else block


def last_kernel(rows, starts, nx, n_in, pos, spring, vec, heat, partial, self_in, counts,
                own_high, own_low, *rest):
    received = rest[:n_in]
    v2, h2, v3, h3, pool, far_high, far_low, edge_high, edge_low = rest[n_in:]

    def body(row):
        for j, place in enumerate(row):
            pool[j] = block_at(received, starts, place)

    for_each_row(rows, nx, body)
    values = {s: pool[j] for j, s in enumerate(WIDE)}
    halves = {s: split(x) for s, x in values.items()}
    geo = jnp.concatenate(
        [values[s][0:4] for s in WIDE] + [jnp.zeros((A - 4 * len(WIDE), A), F32)], axis=0
    ).T[3 * G :]
    geo = {
        s: [
            jnp.sqrt(geo[:, 4 * j + c : 4 * j + c + 1]) if c == 3 else geo[:, 4 * j + c : 4 * j + c + 1]
            for c in range(4)
        ]
        for j, s in enumerate(WIDE)
    }
    wide_geo = {s: spread(x) for s, x in geo.items()}

    def shifted(cols, s):
        return [cols[0] + column_edge * s[0], cols[1] + column_edge * s[1], cols[2], cols[3]]

    quads = (RING[:4], RING[4:])
    sides = []
    for q, quad in enumerate(quads):
        blocks = [[pool[len(WIDE) + k * 8 + 4 * q + g] for g in range(4)] for k in range(2)]
        fields = [by_group([moved(values[s], b, g) for g, s in enumerate(quad)]) for b in range(3)]
        begun = [by_group([moved(x, b, g) for g, x in enumerate(blocks[0])]) for b in range(3)]
        sides.append((quad, fields, begun, blocks))

    home = spread([pos[0], pos[1], pos[2], jnp.sqrt(spring[...])])
    sums = {}
    for j, s in enumerate(RING):
        terms = pair_terms(counts[j], shifted(wide_geo[s], s), home)
        put_terms(far_high, far_low, sums, [b * 2 * A + j * G for b in range(3)], terms)
    far_terms = total(sums)

    def beside(first, second):
        return jnp.concatenate([x for b in range(3) for x in (first[b], second[b])], axis=1)

    current = stacked(vec, heat)
    far = apply_weights(far_high, far_low, beside(sides[0][1], sides[1][1]))
    second = []
    for a in range(3):
        inner = self_product(far_terms, current, a) - far[:, a * A : (a + 1) * A]
        second.append(partial[a] + 2.0 * inner)
        v2[a] = second[a][:8]
        h2[a] = second[a][8:]

    for j in range(len(RING)):
        edge_high[j * A + 3 * G : (j + 1) * A, :] = jnp.zeros((G, OWN), BF16)
        edge_low[j * A + 3 * G : (j + 1) * A, :] = jnp.zeros((G, OWN), BF16)
    edges = []
    for quad, fields, begun, blocks in sides:
        lists = [
            by_group([moved(blocks[1 if k < 3 else 0][g], k, g) for g in range(4)]) for k in range(4)
        ]
        counters = count_slots(jnp.concatenate(lists, axis=0).astype(jnp.int32), FAR_GROUPS)
        there = by_group([moved(values[s][0:8], 3, g) for g, s in enumerate(quad)])
        home = spread([there[0:1], there[1:2], there[2:3], jnp.sqrt(there[3:4])])
        sums = {}
        for j, s in enumerate(RING):
            around = [(t[0] + s[0], t[1] + s[1]) for t in quad]
            source = [by_group([wide_geo[t][c] for t in around]) for c in range(4)]
            terms = pair_terms(counters[j], shifted(source, s), home)
            put_terms(edge_high, edge_low, sums, [j * A + b * G for b in range(3)], terms)
        terms = total(sums)
        lhs = [
            jnp.concatenate(
                [
                    jnp.concatenate([halves[(t[0] + s[0], t[1] + s[1])][h] for s in RING], axis=1)
                    for t in quad
                ],
                axis=0,
            )
            for h in range(2)
        ]
        main = jnp.dot(jnp.concatenate(lhs, axis=0), edge_high[...], preferred_element_type=F32)
        small = jnp.dot(lhs[0], edge_low[...], preferred_element_type=F32)
        result = []
        for a in range(3):
            cut = slice(a * A, (a + 1) * A)
            sums_of = [
                main[g * F : (g + 1) * F, cut]
                + main[(4 + g) * F : (5 + g) * F, cut]
                + small[g * F : (g + 1) * F, cut]
                for g in range(4)
            ]
            inner = self_product(terms, fields, a) - by_group(sums_of)
            result.append(begun[a] + 2.0 * inner)
        edges.append(result)

    all_terms = {key: far_terms[key] + self_in[i : i + 1, :] for i, key in enumerate(KEYS)}
    far = apply_weights(far_high, far_low, beside(*edges))
    far += apply_weights(own_high, own_low, jnp.concatenate(second, axis=1))
    for a in range(3):
        inner = self_product(all_terms, second, a) - far[:, a * A : (a + 1) * A] - second[a]
        third = 2.0 * inner - current[a]
        v3[a] = third[:8]
        h3[a] = third[8:]


def call(kernel, out_shape, args, scratch=()):
    size = sum(x.size * x.dtype.itemsize for x in (*args, *out_shape))
    return pl.pallas_call(
        kernel,
        out_shape=out_shape,
        scratch_shapes=scratch,
        cost_estimate=pl.CostEstimate(flops=2**20, bytes_accessed=size, transcendentals=0),
        compiler_params=pltpu.CompilerParams(vmem_limit_bytes=24 * 2**20),
    )(*args)


def shards(positions, spring, border, neighbours, vec_prev, vec_now, heat_prev, heat_now):
    nx, ny = lax.axis_size("gx"), lax.axis_size("gy")
    steps, sizes, starts, send_rows, last_rows, links = make_plan(nx, ny)
    shape = jax.ShapeDtypeStruct
    vector = shape((3, 8, A), F32)
    pos = positions.reshape(3, 1, A)
    stiff = spring.reshape(1, A)
    entries = neighbours.reshape(NB, A)
    v0, v1, h0, h1 = (x.reshape(3, 8, A) for x in (vec_prev, vec_now, heat_prev, heat_now))
    payload, own_high, own_low, partial, self_terms, counts = call(
        own_kernel,
        (
            shape((KINDS, F, A), F32),
            shape((OWN, OWN), BF16),
            shape((OWN, OWN), BF16),
            shape((3, F, A), F32),
            shape((6, A), F32),
            shape((8, 8, A), jnp.int32),
        ),
        (pos, stiff, border.reshape(1, G), entries, v1, h1, v0, h0),
    )
    received = [payload]
    for i, (_, base) in enumerate(steps):
        known = received[: base + 2]
        if send_rows[i][0] == tuple(range(KINDS)) and len(set(send_rows[i].values())) == 1:
            outgoing = payload
        else:
            (outgoing,) = call(
                functools.partial(relay_kernel, send_rows[i], starts, nx),
                (shape((sizes[i], F, A), F32),),
                known,
            )
        received.append(lax.ppermute(outgoing, ("gx", "gy"), links[i]))
    v2, h2, v3, h3 = call(
        functools.partial(last_kernel, last_rows, starts, nx, len(received)),
        (vector,) * 4,
        (pos, stiff, v1, h1, partial, self_terms, counts, own_high, own_low, *received),
        (
            pltpu.VMEM((len(WIDE) + 16, F, A), F32),
            pltpu.VMEM((6 * A, OWN), BF16),
            pltpu.VMEM((6 * A, OWN), BF16),
            pltpu.VMEM((8 * A, OWN), BF16),
            pltpu.VMEM((8 * A, OWN), BF16),
        ),
    )
    whole = vec_prev.shape
    return v2.reshape(whole), v3.reshape(whole), h2.reshape(whole), h3.reshape(whole)


def solution(mesh):
    wide = P(None, None, "gx", "gy", None)
    return jax.shard_map(
        shards,
        mesh=mesh,
        in_specs=(
            P(None, "gx", "gy", None),
            P("gx", "gy", None),
            P("gx", "gy", None),
            P("gx", "gy", None, None),
            wide, wide, wide, wide,
        ),
        out_specs=(wide, wide, wide, wide),
        check_vma=False,
    )
```

```python
import functools

import jax
import jax.numpy as jnp
from jax import lax
from jax.experimental import pallas as pl
from jax.experimental.pallas import tpu as pltpu
from jax.sharding import PartitionSpec as P

column_edge = 20.0
reach_sq = 64.0
A = 128
G = 32
NB = 64
F = 16
OWN = 3 * A
F32 = jnp.float32
BF16 = jnp.bfloat16
KEYS = ((0, 0), (0, 1), (0, 2), (1, 1), (1, 2), (2, 2))
RING = ((-1, -1), (-1, 0), (-1, 1), (0, -1), (0, 1), (1, -1), (1, 0), (1, 1))
WIDE = tuple((x, y) for x in range(-2, 3) for y in range(-2, 3))
KINDS = 3


def other(i, count):
    return (i + 1) % count if i % 2 else (i - 1) % count


def routes(nx, ny):
    def pair_x(x, y):
        return x ^ 1, y

    def pair_y(x, y):
        return x, y ^ 1

    def across(x, y):
        if x in (0, nx - 1):
            return other(x, nx), y
        return x, other(y, ny)

    def beside(x, y):
        if x not in (0, nx - 1):
            return other(x, nx), y
        return (x if y % 4 in (1, 2) else other(x, nx)), other(y, ny)

    return pair_x, pair_y, across, beside, pair_x, pair_y


def class_of(x, y, nx):
    ends = {0: 0, 1: 1, nx - 2: 4, nx - 1: 5}
    return 4 * ends.get(x, 2 + x % 2) + y % 4


@functools.lru_cache(None)
def make_plan(nx, ny):
    devices = [(x, y) for x in range(nx) for y in range(ny)]
    steps = routes(nx, ny)
    source = [{f(*d): d for d in devices} for f in steps]
    known, brought = {d: {d} for d in devices}, []
    for i in range(len(steps)):
        brought.append({d: known[source[i][d]] for d in devices})
        known = {d: known[d] | brought[i][d] for d in devices}

    def wanted(x, y):
        return [
            (kind, (x + a) % nx, (y + b) % ny)
            for kind in range(KINDS)
            for a, b in (WIDE if kind == 0 else RING)
        ]

    def route_of(item, d, before):
        found = [i for i in range(before) if item[1:] in brought[i][d]]
        late = item[0] and item[1] != d[0] and item[2] != d[1]
        return found[-1 if late else 0]

    sent = [{d: set() for d in devices} for _ in steps]

    def ask(items, d, before):
        for item in items:
            if item[1:] != d:
                i = route_of(item, d, before)
                sent[i][d].add(item)

    for d in devices:
        ask(wanted(*d), d, len(steps))
    for i in reversed(range(len(steps))):
        for d in devices:
            ask(sent[i][d], source[i][d], i)

    def order(d):
        near = lambda v, count: (v + count // 2) % count
        return lambda m: (m[0], near(m[1] - d[0], nx), near(m[2] - d[1], ny))

    lists = [{d: sorted(s[d], key=order(d)) for d in devices} for s in sent]
    sizes = [max(1, *map(len, s.values())) for s in lists]
    starts = [KINDS + sum(sizes[:i]) for i in range(len(sizes))]

    def place(item, d, before):
        if item[1:] == d:
            return item[0]
        i = route_of(item, d, before)
        return starts[i] + lists[i][d].index(item)

    send_rows = [{} for _ in steps]
    last_rows = {}
    for d in devices:
        c = class_of(*d, nx)
        for i, f in enumerate(steps):
            row = tuple(place(item, d, i) for item in lists[i][f(*d)])
            assert send_rows[i].setdefault(c, row) == row
        row = tuple(place(item, d, len(steps)) for item in wanted(*d))
        assert last_rows.setdefault(c, row) == row
    links = [[(x * ny + y, f(x, y)[0] * ny + f(x, y)[1]) for x, y in devices] for f in steps]
    return steps, sizes, starts, send_rows, last_rows, links


def for_each_row(rows, nx, body):
    x, y = lax.axis_index("gx"), lax.axis_index("gy")
    column = jnp.where(x < 2, x, jnp.where(x < nx - 2, 2 + lax.rem(x, 2), x + 6 - nx))
    mine = 4 * column + lax.rem(y, 4)
    classes = {}
    for c, row in rows.items():
        classes.setdefault(row, []).append(c)
    for row, members in classes.items():
        hit = mine == members[0]
        for c in members[1:]:
            hit = hit | (mine == c)
        pl.when(hit)(functools.partial(body, row))


def block_at(refs, starts, place):
    if place < KINDS:
        return refs[0][place]
    i = max(j for j in range(len(starts)) if starts[j] <= place)
    return refs[i + 1][place - starts[i]]


def relay_kernel(rows, starts, nx, *refs):
    out = refs[-1]

    def body(row):
        for j, place in enumerate(row):
            out[j] = block_at(refs, starts, place)
        for j in range(len(row), out.shape[0]):
            out[j] = jnp.zeros((F, A), F32)

    for_each_row(rows, nx, body)


def split(x):
    high = x.astype(BF16)
    return high, (x - high.astype(F32)).astype(BF16)


def border_lanes(border, values):
    index = jnp.concatenate([border[...]] * (A // G), axis=1)
    return jnp.take_along_axis(values, jnp.broadcast_to(index, values.shape), axis=1)


def by_group(parts):
    group = lax.broadcasted_iota(jnp.int32, parts[0].shape, 1) // G
    out = parts[3]
    for q in range(3):
        out = jnp.where(group == q, parts[q], out)
    return out


def stacked(vec, heat):
    return [jnp.concatenate([vec[b], heat[b]], axis=0) for b in range(3)]


def count_slots(entries, groups):
    sub = lax.broadcasted_iota(jnp.int32, (8, A), 0)
    counters = [jnp.zeros((8, A), jnp.int32) for _ in groups]
    for n in range(NB):
        e = jnp.broadcast_to(entries[n : n + 1, :], (8, A))
        mark = jnp.where(sub == (e & 7), jnp.left_shift(jnp.int32(1), e & 24), 0)
        which = lax.shift_right_arithmetic(e, 5)
        for i, g in enumerate(groups):
            counters[i] += jnp.where(which == g, mark, 0)
    return counters


FAR_GROUPS = [4 * (3 * (x + 1) + y + 1) for x, y in RING]


def pair_terms(counter, source, home):
    tiles = [lax.shift_right_logical(counter, 8 * q) & 255 for q in range(4)]
    count = jnp.concatenate(tiles, axis=0).astype(F32)
    d = [source[a] - home[a] for a in range(3)]
    r2 = d[0] * d[0] + d[1] * d[1] + d[2] * d[2]
    near = r2 + 1.0
    inverse = (count * (home[3] * source[3])) / ((reach_sq + r2) * near)
    c = inverse * near * (reach_sq / NB)
    bend = inverse * (2.0 * reach_sq / NB)
    g = [bend * d[a] for a in range(3)]
    return {(a, b): (g[a] * d[b] + c if a == b else g[a] * d[b]) for a, b in KEYS}


def put_terms(w_high, w_low, sums, rows, terms):
    for (a, b), value in terms.items():
        part = value[0:8] + value[8:16] + value[16:24] + value[24:32]
        sums[(a, b)] = sums[(a, b)] + part if (a, b) in sums else part
        high, low = split(value)
        for p, q in sorted({(a, b), (b, a)}):
            w_high[rows[q] : rows[q] + G, p * A : (p + 1) * A] = high
            w_low[rows[q] : rows[q] + G, p * A : (p + 1) * A] = low


def total(sums):
    return {key: jnp.sum(value, axis=0, keepdims=True) for key, value in sums.items()}


def apply_weights(w_high, w_low, lhs):
    high, low = split(lhs)
    both = jnp.concatenate([high, low], axis=0)
    main = jnp.dot(both, w_high[...], preferred_element_type=F32)
    rest = jnp.dot(high, w_low[...], preferred_element_type=F32)
    return main[:F] + main[F:] + rest


def self_product(terms, fields, a):
    return sum(terms[(min(a, b), max(a, b))] * fields[b] for b in range(3))


def spread(rows):
    return [jnp.broadcast_to(r, (G, A)) for r in rows]


def own_kernel(*refs):
    inputs, outputs, buffers, arrived = refs[:8], refs[8:16], refs[16:24], refs[24]
    payload, w_high, w_low, partial, self_out, counts, state, place = outputs
    copies = [
        pltpu.make_async_copy(source, target, arrived.at[i])
        for i, (source, target) in enumerate(zip(inputs, buffers))
    ]
    for copy in copies:
        copy.start()
    entries, pos, spring, border, vec, heat, vec0, heat0 = buffers
    copies[0].wait()
    counters = count_slots(entries[...], FAR_GROUPS + [16, 17, 18, 19])
    for i in range(8):
        counts[i] = counters[i]
    for copy in copies[1:]:
        copy.wait()
    root = jnp.sqrt(spring[...])
    home = spread([pos[0], pos[1], pos[2], root])
    place[...] = jnp.concatenate([pos[0], pos[1], pos[2], root, jnp.zeros((4, A), F32)], axis=0)
    geo = place[...].T
    sums = {}
    for t in range(4):
        source = spread([geo[t * G : (t + 1) * G, c : c + 1] for c in range(4)])
        terms = pair_terms(counters[8 + t], source, home)
        put_terms(w_high, w_low, sums, [b * A + t * G for b in range(3)], terms)
    own_terms = total(sums)
    for i, key in enumerate(KEYS):
        self_out[i : i + 1, :] = own_terms[key]
    current, previous = stacked(vec, heat), stacked(vec0, heat0)
    far = apply_weights(w_high, w_low, jnp.concatenate(current, axis=1))
    begun = []
    for a in range(3):
        inner = self_product(own_terms, current, a) - far[:, a * A : (a + 1) * A] - current[a]
        begun.append(2.0 * inner - previous[a])
        partial[a] = begun[a]
        state[a] = current[a]
    geometry = jnp.concatenate(
        [pos[0], pos[1], pos[2], spring[...], jnp.zeros((F - 4, A), F32)], axis=0
    )
    picked = functools.partial(border_lanes, border)
    lists = [picked(entries[F * s : F * (s + 1), :].astype(F32)) for s in range(4)]
    payload[0] = by_group([picked(x) for x in (*current, geometry)])
    payload[1] = by_group([picked(x) for x in begun] + [lists[3]])
    payload[2] = by_group(lists[:3] + [jnp.zeros((F, A), F32)])


def moved(block, source, target):
    shift = (target - source) % 4 * G
    return pltpu.roll(block, shift, 1) if shift else block


def last_kernel(rows, starts, nx, n_in, place, state, partial, self_in, counts,
                own_high, own_low, *rest):
    received = rest[:n_in]
    v2, h2, v3, h3, pool, far_high, far_low, edge_high, edge_low = rest[n_in:]

    def body(row):
        for j, place in enumerate(row):
            pool[j] = block_at(received, starts, place)

    for_each_row(rows, nx, body)
    values = {s: pool[j] for j, s in enumerate(WIDE)}
    halves = {s: split(x) for s, x in values.items()}
    geo = jnp.concatenate(
        [values[s][0:4] for s in WIDE] + [jnp.zeros((A - 4 * len(WIDE), A), F32)], axis=0
    ).T[3 * G :]
    geo = {
        s: [
            jnp.sqrt(geo[:, 4 * j + c : 4 * j + c + 1]) if c == 3 else geo[:, 4 * j + c : 4 * j + c + 1]
            for c in range(4)
        ]
        for j, s in enumerate(WIDE)
    }
    wide_geo = {s: spread(x) for s, x in geo.items()}

    def shifted(cols, s):
        return [cols[0] + column_edge * s[0], cols[1] + column_edge * s[1], cols[2], cols[3]]

    quads = (RING[:4], RING[4:])
    sides = []
    for q, quad in enumerate(quads):
        blocks = [[pool[len(WIDE) + k * 8 + 4 * q + g] for g in range(4)] for k in range(2)]
        fields = [by_group([moved(values[s], b, g) for g, s in enumerate(quad)]) for b in range(3)]
        begun = [by_group([moved(x, b, g) for g, x in enumerate(blocks[0])]) for b in range(3)]
        sides.append((quad, fields, begun, blocks))

    home = spread([place[c : c + 1, :] for c in range(4)])
    sums = {}
    for j, s in enumerate(RING):
        terms = pair_terms(counts[j], shifted(wide_geo[s], s), home)
        put_terms(far_high, far_low, sums, [b * 2 * A + j * G for b in range(3)], terms)
    far_terms = total(sums)

    def beside(first, second):
        return jnp.concatenate([x for b in range(3) for x in (first[b], second[b])], axis=1)

    current = [state[b] for b in range(3)]
    far = apply_weights(far_high, far_low, beside(sides[0][1], sides[1][1]))
    second = []
    for a in range(3):
        inner = self_product(far_terms, current, a) - far[:, a * A : (a + 1) * A]
        second.append(partial[a] + 2.0 * inner)
        v2[a] = second[a][:8]
        h2[a] = second[a][8:]

    for j in range(len(RING)):
        edge_high[j * A + 3 * G : (j + 1) * A, :] = jnp.zeros((G, OWN), BF16)
        edge_low[j * A + 3 * G : (j + 1) * A, :] = jnp.zeros((G, OWN), BF16)
    edges = []
    for quad, fields, begun, blocks in sides:
        lists = [
            by_group([moved(blocks[1 if k < 3 else 0][g], k, g) for g in range(4)]) for k in range(4)
        ]
        counters = count_slots(jnp.concatenate(lists, axis=0).astype(jnp.int32), FAR_GROUPS)
        there = by_group([moved(values[s][0:8], 3, g) for g, s in enumerate(quad)])
        home = spread([there[0:1], there[1:2], there[2:3], jnp.sqrt(there[3:4])])
        sums = {}
        for j, s in enumerate(RING):
            around = [(t[0] + s[0], t[1] + s[1]) for t in quad]
            source = [by_group([wide_geo[t][c] for t in around]) for c in range(4)]
            terms = pair_terms(counters[j], shifted(source, s), home)
            put_terms(edge_high, edge_low, sums, [j * A + b * G for b in range(3)], terms)
        terms = total(sums)
        lhs = [
            jnp.concatenate(
                [
                    jnp.concatenate([halves[(t[0] + s[0], t[1] + s[1])][h] for s in RING], axis=1)
                    for t in quad
                ],
                axis=0,
            )
            for h in range(2)
        ]
        main = jnp.dot(jnp.concatenate(lhs, axis=0), edge_high[...], preferred_element_type=F32)
        small = jnp.dot(lhs[0], edge_low[...], preferred_element_type=F32)
        result = []
        for a in range(3):
            cut = slice(a * A, (a + 1) * A)
            sums_of = [
                main[g * F : (g + 1) * F, cut]
                + main[(4 + g) * F : (5 + g) * F, cut]
                + small[g * F : (g + 1) * F, cut]
                for g in range(4)
            ]
            inner = self_product(terms, fields, a) - by_group(sums_of)
            result.append(begun[a] + 2.0 * inner)
        edges.append(result)

    all_terms = {key: far_terms[key] + self_in[i : i + 1, :] for i, key in enumerate(KEYS)}
    far = apply_weights(far_high, far_low, beside(*edges))
    far += apply_weights(own_high, own_low, jnp.concatenate(second, axis=1))
    for a in range(3):
        inner = self_product(all_terms, second, a) - far[:, a * A : (a + 1) * A] - second[a]
        third = 2.0 * inner - current[a]
        v3[a] = third[:8]
        h3[a] = third[8:]


def call(kernel, name, out_shape, args, scratch=(), space=pltpu.VMEM):
    size = sum(x.size * x.dtype.itemsize for x in (*args, *out_shape))
    return pl.pallas_call(
        kernel,
        out_shape=out_shape,
        in_specs=[pl.BlockSpec(memory_space=space)] * len(args),
        scratch_shapes=scratch,
        name=name,
        cost_estimate=pl.CostEstimate(flops=2**20, bytes_accessed=size, transcendentals=0),
        compiler_params=pltpu.CompilerParams(vmem_limit_bytes=24 * 2**20),
    )(*args)


def shards(positions, spring, border, neighbours, vec_prev, vec_now, heat_prev, heat_now):
    nx, ny = lax.axis_size("gx"), lax.axis_size("gy")
    steps, sizes, starts, send_rows, last_rows, links = make_plan(nx, ny)
    shape = jax.ShapeDtypeStruct
    vector = shape((3, 8, A), F32)
    pos = positions.reshape(3, 1, A)
    stiff = spring.reshape(1, A)
    entries = neighbours.reshape(NB, A)
    v0, v1, h0, h1 = (x.reshape(3, 8, A) for x in (vec_prev, vec_now, heat_prev, heat_now))
    first = [
        pltpu.with_memory_space_constraint(x, pltpu.HBM)
        for x in (entries, pos, stiff, border.reshape(1, G), v1, h1, v0, h0)
    ]
    payload, own_high, own_low, partial, self_terms, counts, state, place = call(
        own_kernel,
        "own_kernel",
        (
            shape((KINDS, F, A), F32),
            shape((OWN, OWN), BF16),
            shape((OWN, OWN), BF16),
            shape((3, F, A), F32),
            shape((6, A), F32),
            shape((8, 8, A), jnp.int32),
            shape((3, F, A), F32),
            shape((8, A), F32),
        ),
        first,
        [pltpu.VMEM(x.shape, x.dtype) for x in first] + [pltpu.SemaphoreType.DMA((8,))],
        pltpu.HBM,
    )
    received = [payload]
    for i in range(len(steps)):
        if send_rows[i][0] == tuple(range(KINDS)) and len(set(send_rows[i].values())) == 1:
            outgoing = payload
        else:
            (outgoing,) = call(
                functools.partial(relay_kernel, send_rows[i], starts, nx),
                f"relay_{i}",
                (shape((sizes[i], F, A), F32),),
                received,
            )
        received.append(lax.ppermute(outgoing, ("gx", "gy"), links[i]))
    v2, h2, v3, h3 = call(
        functools.partial(last_kernel, last_rows, starts, nx, len(received)),
        "last_kernel",
        (vector,) * 4,
        (place, state, partial, self_terms, counts, own_high, own_low, *received),
        (
            pltpu.VMEM((len(WIDE) + 16, F, A), F32),
            pltpu.VMEM((6 * A, OWN), BF16),
            pltpu.VMEM((6 * A, OWN), BF16),
            pltpu.VMEM((8 * A, OWN), BF16),
            pltpu.VMEM((8 * A, OWN), BF16),
        ),
    )
    whole = vec_prev.shape
    return v2.reshape(whole), v3.reshape(whole), h2.reshape(whole), h3.reshape(whole)


def solution(mesh):
    wide = P(None, None, "gx", "gy", None)
    return jax.shard_map(
        shards,
        mesh=mesh,
        in_specs=(
            P(None, "gx", "gy", None),
            P("gx", "gy", None),
            P("gx", "gy", None),
            P("gx", "gy", None, None),
            wide, wide, wide, wide,
        ),
        out_specs=(wide, wide, wide, wide),
        check_vma=False,
    )
```

```python
import functools

import jax
import jax.numpy as jnp
from jax import lax
from jax.experimental import pallas as pl
from jax.experimental.pallas import tpu as pltpu
from jax.sharding import PartitionSpec as P

column_edge = 20.0
reach_sq = 64.0
A = 128
G = 32
NB = 64
F = 16
OWN = 3 * A
F32 = jnp.float32
BF16 = jnp.bfloat16
KEYS = ((0, 0), (0, 1), (0, 2), (1, 1), (1, 2), (2, 2))
RING = ((-1, -1), (-1, 0), (-1, 1), (0, -1), (0, 1), (1, -1), (1, 0), (1, 1))
WIDE = tuple((x, y) for x in range(-2, 3) for y in range(-2, 3))
KINDS = 3


def other(i, count):
    return (i + 1) % count if i % 2 else (i - 1) % count


def routes(nx, ny):
    def pair_x(x, y):
        return x ^ 1, y

    def pair_y(x, y):
        return x, y ^ 1

    def across(x, y):
        if x in (0, nx - 1):
            return other(x, nx), y
        return x, other(y, ny)

    def beside(x, y):
        if x not in (0, nx - 1):
            return other(x, nx), y
        return (x if y % 4 in (1, 2) else other(x, nx)), other(y, ny)

    return pair_x, pair_y, across, beside, pair_x, pair_y


def class_of(x, y, nx):
    ends = {0: 0, 1: 1, nx - 2: 4, nx - 1: 5}
    return 4 * ends.get(x, 2 + x % 2) + y % 4


@functools.lru_cache(None)
def make_plan(nx, ny):
    devices = [(x, y) for x in range(nx) for y in range(ny)]
    steps = routes(nx, ny)
    source = [{f(*d): d for d in devices} for f in steps]
    known, brought = {d: {d} for d in devices}, []
    for i in range(len(steps)):
        brought.append({d: known[source[i][d]] for d in devices})
        known = {d: known[d] | brought[i][d] for d in devices}

    def wanted(x, y):
        return [
            (kind, (x + a) % nx, (y + b) % ny)
            for kind in range(KINDS)
            for a, b in (WIDE if kind == 0 else RING)
        ]

    def route_of(item, d, before):
        found = [i for i in range(before) if item[1:] in brought[i][d]]
        late = item[0] and item[1] != d[0] and item[2] != d[1]
        return found[-1 if late else 0]

    sent = [{d: set() for d in devices} for _ in steps]

    def ask(items, d, before):
        for item in items:
            if item[1:] != d:
                i = route_of(item, d, before)
                sent[i][d].add(item)

    for d in devices:
        ask(wanted(*d), d, len(steps))
    for i in reversed(range(len(steps))):
        for d in devices:
            ask(sent[i][d], source[i][d], i)

    def order(d):
        near = lambda v, count: (v + count // 2) % count
        return lambda m: (m[0], near(m[1] - d[0], nx), near(m[2] - d[1], ny))

    lists = [{d: sorted(s[d], key=order(d)) for d in devices} for s in sent]
    sizes = [max(1, *map(len, s.values())) for s in lists]
    starts = [KINDS + sum(sizes[:i]) for i in range(len(sizes))]

    def place(item, d, before):
        if item[1:] == d:
            return item[0]
        i = route_of(item, d, before)
        return starts[i] + lists[i][d].index(item)

    send_rows = [{} for _ in steps]
    last_rows, next_rows = {}, {}
    for d in devices:
        c = class_of(*d, nx)
        for i, f in enumerate(steps):
            row = tuple(place(item, d, i) for item in lists[i][f(*d)])
            assert send_rows[i].setdefault(c, row) == row
        row = tuple(place(item, d, len(steps)) for item in wanted(*d))
        assert last_rows.setdefault(c, row) == row
        row = tuple(row[WIDE.index(s)] for s in RING)
        assert max(row) < starts[-1] and next_rows.setdefault(c, row) == row
    links = [[(x * ny + y, f(x, y)[0] * ny + f(x, y)[1]) for x, y in devices] for f in steps]
    return steps, sizes, starts, send_rows, next_rows, last_rows, links


def for_each_row(rows, nx, body):
    x, y = lax.axis_index("gx"), lax.axis_index("gy")
    column = jnp.where(x < 2, x, jnp.where(x < nx - 2, 2 + lax.rem(x, 2), x + 6 - nx))
    mine = 4 * column + lax.rem(y, 4)
    classes = {}
    for c, row in rows.items():
        classes.setdefault(row, []).append(c)
    for row, members in classes.items():
        hit = mine == members[0]
        for c in members[1:]:
            hit = hit | (mine == c)
        pl.when(hit)(functools.partial(body, row))


def block_at(refs, starts, place):
    if place < KINDS:
        return refs[0][place]
    i = max(j for j in range(len(starts)) if starts[j] <= place)
    return refs[i + 1][place - starts[i]]


def relay_kernel(rows, starts, nx, *refs):
    out = refs[-1]

    def body(row):
        for j, place in enumerate(row):
            out[j] = block_at(refs, starts, place)
        for j in range(len(row), out.shape[0]):
            out[j] = jnp.zeros((F, A), F32)

    for_each_row(rows, nx, body)


def split(x):
    high = x.astype(BF16)
    return high, (x - high.astype(F32)).astype(BF16)


def border_lanes(border, values):
    index = jnp.concatenate([border[...]] * (A // G), axis=1)
    return jnp.take_along_axis(values, jnp.broadcast_to(index, values.shape), axis=1)


def by_group(parts):
    group = lax.broadcasted_iota(jnp.int32, parts[0].shape, 1) // G
    out = parts[3]
    for q in range(3):
        out = jnp.where(group == q, parts[q], out)
    return out


def stacked(vec, heat):
    return [jnp.concatenate([vec[b], heat[b]], axis=0) for b in range(3)]


def count_slots(entries, groups):
    sub = lax.broadcasted_iota(jnp.int32, (8, A), 0)
    counters = [jnp.zeros((8, A), jnp.int32) for _ in groups]
    for n in range(NB):
        e = jnp.broadcast_to(entries[n : n + 1, :], (8, A))
        mark = jnp.where(sub == (e & 7), jnp.left_shift(jnp.int32(1), e & 24), 0)
        which = lax.shift_right_arithmetic(e, 5)
        for i, g in enumerate(groups):
            counters[i] += jnp.where(which == g, mark, 0)
    return counters


FAR_GROUPS = [4 * (3 * (x + 1) + y + 1) for x, y in RING]


def pair_terms(counter, source, home):
    tiles = [lax.shift_right_logical(counter, 8 * q) & 255 for q in range(4)]
    count = jnp.concatenate(tiles, axis=0).astype(F32)
    d = [source[a] - home[a] for a in range(3)]
    r2 = d[0] * d[0] + d[1] * d[1] + d[2] * d[2]
    near = r2 + 1.0
    inverse = (count * (home[3] * source[3])) / ((reach_sq + r2) * near)
    c = inverse * near * (reach_sq / NB)
    bend = inverse * (2.0 * reach_sq / NB)
    g = [bend * d[a] for a in range(3)]
    return {(a, b): (g[a] * d[b] + c if a == b else g[a] * d[b]) for a, b in KEYS}


def put_terms(w_high, w_low, sums, rows, terms):
    for (a, b), value in terms.items():
        part = value[0:8] + value[8:16] + value[16:24] + value[24:32]
        sums[(a, b)] = sums[(a, b)] + part if (a, b) in sums else part
        high, low = split(value)
        for p, q in sorted({(a, b), (b, a)}):
            w_high[rows[q] : rows[q] + G, p * A : (p + 1) * A] = high
            w_low[rows[q] : rows[q] + G, p * A : (p + 1) * A] = low


def total(sums):
    return {key: jnp.sum(value, axis=0, keepdims=True) for key, value in sums.items()}


def apply_weights(w_high, w_low, lhs):
    high, low = split(lhs)
    both = jnp.concatenate([high, low], axis=0)
    main = jnp.dot(both, w_high[...], preferred_element_type=F32)
    rest = jnp.dot(high, w_low[...], preferred_element_type=F32)
    return main[:F] + main[F:] + rest


def self_product(terms, fields, a):
    return sum(terms[(min(a, b), max(a, b))] * fields[b] for b in range(3))


def spread(rows):
    return [jnp.broadcast_to(r, (G, A)) for r in rows]


def own_kernel(*refs):
    inputs, outputs, buffers, arrived = refs[:8], refs[8:16], refs[16:24], refs[24]
    payload, w_high, w_low, partial, self_out, counts, state, place = outputs
    copies = [
        pltpu.make_async_copy(source, target, arrived.at[i])
        for i, (source, target) in enumerate(zip(inputs, buffers))
    ]
    for copy in copies:
        copy.start()
    entries, pos, spring, border, vec, heat, vec0, heat0 = buffers
    copies[0].wait()
    counters = count_slots(entries[...], FAR_GROUPS + [16, 17, 18, 19])
    for i in range(8):
        counts[i] = counters[i]
    for copy in copies[1:]:
        copy.wait()
    root = jnp.sqrt(spring[...])
    home = spread([pos[0], pos[1], pos[2], root])
    place[...] = jnp.concatenate([pos[0], pos[1], pos[2], root, jnp.zeros((4, A), F32)], axis=0)
    geo = place[...].T
    sums = {}
    for t in range(4):
        source = spread([geo[t * G : (t + 1) * G, c : c + 1] for c in range(4)])
        terms = pair_terms(counters[8 + t], source, home)
        put_terms(w_high, w_low, sums, [b * A + t * G for b in range(3)], terms)
    own_terms = total(sums)
    for i, key in enumerate(KEYS):
        self_out[i : i + 1, :] = own_terms[key]
    current, previous = stacked(vec, heat), stacked(vec0, heat0)
    far = apply_weights(w_high, w_low, jnp.concatenate(current, axis=1))
    begun = []
    for a in range(3):
        inner = self_product(own_terms, current, a) - far[:, a * A : (a + 1) * A] - current[a]
        begun.append(2.0 * inner - previous[a])
        partial[a] = begun[a]
        state[a] = current[a]
    geometry = jnp.concatenate(
        [pos[0], pos[1], pos[2], spring[...], jnp.zeros((F - 4, A), F32)], axis=0
    )
    picked = functools.partial(border_lanes, border)
    lists = [picked(entries[F * s : F * (s + 1), :].astype(F32)) for s in range(4)]
    payload[0] = by_group([picked(x) for x in (*current, geometry)])
    payload[1] = by_group([picked(x) for x in begun] + [lists[3]])
    payload[2] = by_group(lists[:3] + [jnp.zeros((F, A), F32)])


def moved(block, source, target):
    shift = (target - source) % 4 * G
    return pltpu.roll(block, shift, 1) if shift else block


def geometry_of(values):
    rows = [v[0:4] for v in values.values()]
    rows.append(jnp.zeros((A - 4 * len(values), A), F32))
    geo = jnp.concatenate(rows, axis=0).T[3 * G :]
    out = {}
    for j, s in enumerate(values):
        cols = [geo[:, 4 * j + c : 4 * j + c + 1] for c in range(4)]
        out[s] = spread(cols[:3] + [jnp.sqrt(cols[3])])
    return out


def shifted(cols, s):
    return [cols[0] + column_edge * s[0], cols[1] + column_edge * s[1], cols[2], cols[3]]


def fill_pool(rows, starts, nx, received, pool):
    def body(row):
        for j, place in enumerate(row):
            pool[j] = block_at(received, starts, place)

    for_each_row(rows, nx, body)


QUADS = (RING[:4], RING[4:])


def side_fields(values):
    return [
        [by_group([moved(values[s], b, g) for g, s in enumerate(quad)]) for b in range(3)]
        for quad in QUADS
    ]


def woven(first, second):
    return jnp.concatenate([x for b in range(3) for x in (first[b], second[b])], axis=1)


def next_kernel(rows, starts, nx, n_in, place, state, partial, self_in, counts,
                own_high, own_low, *rest):
    v2, h2, begun, far_high, far_low, pool = rest[n_in:]
    fill_pool(rows, starts, nx, rest[:n_in], pool)
    values = {s: pool[j] for j, s in enumerate(RING)}
    geo = geometry_of(values)
    home = spread([place[c : c + 1, :] for c in range(4)])
    sums = {}
    for j, s in enumerate(RING):
        terms = pair_terms(counts[j], shifted(geo[s], s), home)
        put_terms(far_high, far_low, sums, [b * 2 * A + j * G for b in range(3)], terms)
    far_terms = total(sums)
    current = [state[b] for b in range(3)]
    far = apply_weights(far_high, far_low, woven(*side_fields(values)))
    second = []
    for a in range(3):
        inner = self_product(far_terms, current, a) - far[:, a * A : (a + 1) * A]
        second.append(partial[a] + 2.0 * inner)
        v2[a] = second[a][:8]
        h2[a] = second[a][8:]
    all_terms = {key: far_terms[key] + self_in[i : i + 1, :] for i, key in enumerate(KEYS)}
    far = apply_weights(own_high, own_low, jnp.concatenate(second, axis=1))
    for a in range(3):
        inner = self_product(all_terms, second, a) - far[:, a * A : (a + 1) * A] - second[a]
        begun[a] = 2.0 * inner - current[a]


def last_kernel(rows, starts, nx, n_in, third, far_high, far_low, *rest):
    v3, h3, pool, edge_high, edge_low = rest[n_in:]
    fill_pool(rows, starts, nx, rest[:n_in], pool)
    values = {s: pool[j] for j, s in enumerate(WIDE)}
    halves = {s: split(x) for s, x in values.items()}
    geo = geometry_of(values)
    for j in range(len(RING)):
        edge_high[j * A + 3 * G : (j + 1) * A, :] = jnp.zeros((G, OWN), BF16)
        edge_low[j * A + 3 * G : (j + 1) * A, :] = jnp.zeros((G, OWN), BF16)
    edges = []
    for q, (quad, fields) in enumerate(zip(QUADS, side_fields(values))):
        blocks = [[pool[len(WIDE) + k * 8 + 4 * q + g] for g in range(4)] for k in range(2)]
        begun = [by_group([moved(x, b, g) for g, x in enumerate(blocks[0])]) for b in range(3)]
        lists = [
            by_group([moved(blocks[1 if k < 3 else 0][g], k, g) for g in range(4)]) for k in range(4)
        ]
        counters = count_slots(jnp.concatenate(lists, axis=0).astype(jnp.int32), FAR_GROUPS)
        there = by_group([moved(values[s][0:8], 3, g) for g, s in enumerate(quad)])
        home = spread([there[0:1], there[1:2], there[2:3], jnp.sqrt(there[3:4])])
        sums = {}
        for j, s in enumerate(RING):
            around = [(t[0] + s[0], t[1] + s[1]) for t in quad]
            source = [by_group([geo[t][c] for t in around]) for c in range(4)]
            terms = pair_terms(counters[j], shifted(source, s), home)
            put_terms(edge_high, edge_low, sums, [j * A + b * G for b in range(3)], terms)
        terms = total(sums)
        lhs = [
            jnp.concatenate(
                [
                    jnp.concatenate([halves[(t[0] + s[0], t[1] + s[1])][h] for s in RING], axis=1)
                    for t in quad
                ],
                axis=0,
            )
            for h in range(2)
        ]
        main = jnp.dot(jnp.concatenate(lhs, axis=0), edge_high[...], preferred_element_type=F32)
        small = jnp.dot(lhs[0], edge_low[...], preferred_element_type=F32)
        result = []
        for a in range(3):
            cut = slice(a * A, (a + 1) * A)
            sums_of = [
                main[g * F : (g + 1) * F, cut]
                + main[(4 + g) * F : (5 + g) * F, cut]
                + small[g * F : (g + 1) * F, cut]
                for g in range(4)
            ]
            inner = self_product(terms, fields, a) - by_group(sums_of)
            result.append(begun[a] + 2.0 * inner)
        edges.append(result)
    far = apply_weights(far_high, far_low, woven(*edges))
    for a in range(3):
        result = third[a] - 2.0 * far[:, a * A : (a + 1) * A]
        v3[a] = result[:8]
        h3[a] = result[8:]


def call(kernel, name, out_shape, args, scratch=(), space=pltpu.VMEM):
    size = sum(x.size * x.dtype.itemsize for x in (*args, *out_shape))
    return pl.pallas_call(
        kernel,
        out_shape=out_shape,
        in_specs=[pl.BlockSpec(memory_space=space)] * len(args),
        scratch_shapes=scratch,
        name=name,
        cost_estimate=pl.CostEstimate(flops=2**20, bytes_accessed=size, transcendentals=0),
        compiler_params=pltpu.CompilerParams(vmem_limit_bytes=24 * 2**20),
    )(*args)


def shards(positions, spring, border, neighbours, vec_prev, vec_now, heat_prev, heat_now):
    nx, ny = lax.axis_size("gx"), lax.axis_size("gy")
    steps, sizes, starts, send_rows, next_rows, last_rows, links = make_plan(nx, ny)
    shape = jax.ShapeDtypeStruct
    vector = shape((3, 8, A), F32)
    pos = positions.reshape(3, 1, A)
    stiff = spring.reshape(1, A)
    entries = neighbours.reshape(NB, A)
    v0, v1, h0, h1 = (x.reshape(3, 8, A) for x in (vec_prev, vec_now, heat_prev, heat_now))
    first = [
        pltpu.with_memory_space_constraint(x, pltpu.HBM)
        for x in (entries, pos, stiff, border.reshape(1, G), v1, h1, v0, h0)
    ]
    payload, own_high, own_low, partial, self_terms, counts, state, place = call(
        own_kernel,
        "own_kernel",
        (
            shape((KINDS, F, A), F32),
            shape((OWN, OWN), BF16),
            shape((OWN, OWN), BF16),
            shape((3, F, A), F32),
            shape((6, A), F32),
            shape((8, 8, A), jnp.int32),
            shape((3, F, A), F32),
            shape((8, A), F32),
        ),
        first,
        [pltpu.VMEM(x.shape, x.dtype) for x in first] + [pltpu.SemaphoreType.DMA((8,))],
        pltpu.HBM,
    )
    received = [payload]
    for i in range(len(steps)):
        if send_rows[i][0] == tuple(range(KINDS)) and len(set(send_rows[i].values())) == 1:
            outgoing = payload
        else:
            (outgoing,) = call(
                functools.partial(relay_kernel, send_rows[i], starts, nx),
                f"relay_{i}",
                (shape((sizes[i], F, A), F32),),
                received,
            )
        received.append(lax.ppermute(outgoing, ("gx", "gy"), links[i]))
    early = received[:-1]
    v2, h2, third, far_high, far_low = call(
        functools.partial(next_kernel, next_rows, starts, nx, len(early)),
        "next_kernel",
        (
            vector,
            vector,
            shape((3, F, A), F32),
            shape((6 * A, OWN), BF16),
            shape((6 * A, OWN), BF16),
        ),
        (place, state, partial, self_terms, counts, own_high, own_low, *early),
        (pltpu.VMEM((len(RING), F, A), F32),),
    )
    v3, h3 = call(
        functools.partial(last_kernel, last_rows, starts, nx, len(received)),
        "last_kernel",
        (vector, vector),
        (third, far_high, far_low, *received),
        (
            pltpu.VMEM((len(WIDE) + 16, F, A), F32),
            pltpu.VMEM((8 * A, OWN), BF16),
            pltpu.VMEM((8 * A, OWN), BF16),
        ),
    )
    whole = vec_prev.shape
    return v2.reshape(whole), v3.reshape(whole), h2.reshape(whole), h3.reshape(whole)


def solution(mesh):
    wide = P(None, None, "gx", "gy", None)
    return jax.shard_map(
        shards,
        mesh=mesh,
        in_specs=(
            P(None, "gx", "gy", None),
            P("gx", "gy", None),
            P("gx", "gy", None),
            P("gx", "gy", None, None),
            wide, wide, wide, wide,
        ),
        out_specs=(wide, wide, wide, wide),
        check_vma=False,
    )
```

```python
import functools

import jax
import jax.numpy as jnp
from jax import lax
from jax.experimental import pallas as pl
from jax.experimental.pallas import tpu as pltpu
from jax.sharding import PartitionSpec as P

column_edge = 20.0
reach_sq = 64.0
A = 128
G = 32
NB = 64
F = 16
OWN = 3 * A
F32 = jnp.float32
BF16 = jnp.bfloat16
KEYS = ((0, 0), (0, 1), (0, 2), (1, 1), (1, 2), (2, 2))
EARLY = ((-1, -1), (0, -1), (-1, 0), (1, 0))
LATE = ((1, -1), (-1, 1), (0, 1), (1, 1))
RING = EARLY + LATE
WIDE = tuple((x, y) for x in range(-2, 3) for y in range(-2, 3))
KNOWN = tuple(s for s in WIDE if s[1] < 2)
KINDS = 3


def other(i, count):
    return (i + 1) % count if i % 2 else (i - 1) % count


def routes(nx, ny):
    def pair_x(x, y):
        return x ^ 1, y

    def pair_y(x, y):
        return x, y ^ 1

    def across(x, y):
        if x in (0, nx - 1):
            return other(x, nx), y
        return x, other(y, ny)

    def beside(x, y):
        if x not in (0, nx - 1):
            return other(x, nx), y
        return (x if y % 4 in (1, 2) else other(x, nx)), other(y, ny)

    return pair_x, pair_y, across, beside, pair_x, pair_y


def class_of(x, y, nx):
    ends = {0: 0, 1: 1, nx - 2: 4, nx - 1: 5}
    return 4 * ends.get(x, 2 + x % 2) + y % 4


@functools.lru_cache(None)
def make_plan(nx, ny):
    devices = [(x, y) for x in range(nx) for y in range(ny)]
    steps = routes(nx, ny)
    source = [{f(*d): d for d in devices} for f in steps]
    known, brought = {d: {d} for d in devices}, []
    for i in range(len(steps)):
        brought.append({d: known[source[i][d]] for d in devices})
        known = {d: known[d] | brought[i][d] for d in devices}

    def at(kind, d, steps_to):
        up = 1 - d[1] % 2 * 2
        return [(kind, (d[0] + a) % nx, (d[1] + up * b) % ny) for a, b in steps_to]

    def wanted(d, wide, quad):
        return at(0, d, wide) + at(1, d, quad) + at(2, d, quad)

    soon = {d: at(1, d, EARLY) + at(2, d, EARLY) for d in devices}

    def route_of(item, d, before):
        found = [i for i in range(before) if item[1:] in brought[i][d]]
        if item in soon[d]:
            found = [i for i in found if i < len(steps) - 1]
        late = item[0] and item[1] != d[0] and item[2] != d[1]
        return found[-1 if late else 0]

    sent = [{d: set() for d in devices} for _ in steps]

    def ask(items, d, before):
        for item in items:
            if item[1:] != d:
                i = route_of(item, d, before)
                sent[i][d].add(item)

    for d in devices:
        ask(wanted(d, WIDE, RING), d, len(steps))
    for i in reversed(range(len(steps))):
        for d in devices:
            ask(sent[i][d], source[i][d], i)

    def order(d):
        near = lambda v, count: (v + count // 2) % count
        return lambda m: (m[0], near(m[1] - d[0], nx), near(m[2] - d[1], ny))

    lists = [{d: sorted(s[d], key=order(d)) for d in devices} for s in sent]
    sizes = [max(1, *map(len, s.values())) for s in lists]
    starts = [KINDS + sum(sizes[:i]) for i in range(len(sizes))]

    def place(item, d, before):
        if item[1:] == d:
            return item[0]
        i = route_of(item, d, before)
        return starts[i] + lists[i][d].index(item)

    send_rows = [{} for _ in steps]
    last_rows, next_rows = {}, {}
    for d in devices:
        c = class_of(*d, nx)
        for i, f in enumerate(steps):
            row = tuple(place(item, d, i) for item in lists[i][f(*d)])
            assert send_rows[i].setdefault(c, row) == row
        row = tuple(place(item, d, len(steps)) for item in wanted(d, WIDE, LATE))
        assert last_rows.setdefault(c, row) == row
        row = tuple(place(item, d, len(steps)) for item in wanted(d, KNOWN, EARLY))
        assert max(row) < starts[-1] and next_rows.setdefault(c, row) == row
    links = [[(x * ny + y, f(x, y)[0] * ny + f(x, y)[1]) for x, y in devices] for f in steps]
    return steps, sizes, starts, send_rows, next_rows, last_rows, links


def for_each_row(rows, nx, body):
    x, y = lax.axis_index("gx"), lax.axis_index("gy")
    column = jnp.where(x < 2, x, jnp.where(x < nx - 2, 2 + lax.rem(x, 2), x + 6 - nx))
    mine = 4 * column + lax.rem(y, 4)
    classes = {}
    for c, row in rows.items():
        classes.setdefault(row, []).append(c)
    for row, members in classes.items():
        hit = mine == members[0]
        for c in members[1:]:
            hit = hit | (mine == c)
        pl.when(hit)(functools.partial(body, row))


def block_at(refs, starts, place):
    if place < KINDS:
        return refs[0][place]
    i = max(j for j in range(len(starts)) if starts[j] <= place)
    return refs[i + 1][place - starts[i]]


def relay_kernel(rows, starts, nx, *refs):
    out = refs[-1]

    def body(row):
        for j, place in enumerate(row):
            out[j] = block_at(refs, starts, place)
        for j in range(len(row), out.shape[0]):
            out[j] = jnp.zeros((F, A), F32)

    for_each_row(rows, nx, body)


def split(x):
    high = x.astype(BF16)
    return high, (x - high.astype(F32)).astype(BF16)


def border_lanes(border, values):
    index = jnp.concatenate([border[...]] * (A // G), axis=1)
    return jnp.take_along_axis(values, jnp.broadcast_to(index, values.shape), axis=1)


def by_group(parts):
    group = lax.broadcasted_iota(jnp.int32, parts[0].shape, 1) // G
    out = parts[3]
    for q in range(3):
        out = jnp.where(group == q, parts[q], out)
    return out


def stacked(vec, heat):
    return [jnp.concatenate([vec[b], heat[b]], axis=0) for b in range(3)]


def count_slots(entries, groups):
    sub = lax.broadcasted_iota(jnp.int32, (8, A), 0)
    counters = [jnp.zeros((8, A), jnp.int32) for _ in groups]
    for n in range(NB):
        e = jnp.broadcast_to(entries[n : n + 1, :], (8, A))
        mark = jnp.where(sub == (e & 7), jnp.left_shift(jnp.int32(1), e & 24), 0)
        which = lax.shift_right_arithmetic(e, 5)
        for i, g in enumerate(groups):
            counters[i] += jnp.where(which == g, mark, 0)
    return counters


def upward():
    return 1 - 2 * lax.rem(lax.axis_index("gy"), 2)


def far_groups():
    up = upward()
    return [4 * (3 * (x + 1) + up * y + 1) for x, y in RING]


def pair_terms(counter, source, home):
    tiles = [lax.shift_right_logical(counter, 8 * q) & 255 for q in range(4)]
    count = jnp.concatenate(tiles, axis=0).astype(F32)
    d = [source[a] - home[a] for a in range(3)]
    r2 = d[0] * d[0] + d[1] * d[1] + d[2] * d[2]
    near = r2 + 1.0
    inverse = (count * (home[3] * source[3])) / ((reach_sq + r2) * near)
    c = inverse * near * (reach_sq / NB)
    bend = inverse * (2.0 * reach_sq / NB)
    g = [bend * d[a] for a in range(3)]
    return {(a, b): (g[a] * d[b] + c if a == b else g[a] * d[b]) for a, b in KEYS}


def put_terms(w_high, w_low, sums, rows, terms):
    for (a, b), value in terms.items():
        part = value[0:8] + value[8:16] + value[16:24] + value[24:32]
        sums[(a, b)] = sums[(a, b)] + part if (a, b) in sums else part
        high, low = split(value)
        for p, q in sorted({(a, b), (b, a)}):
            w_high[rows[q] : rows[q] + G, p * A : (p + 1) * A] = high
            w_low[rows[q] : rows[q] + G, p * A : (p + 1) * A] = low


def total(sums):
    return {key: jnp.sum(value, axis=0, keepdims=True) for key, value in sums.items()}


def apply_weights(w_high, w_low, lhs):
    high, low = split(lhs)
    both = jnp.concatenate([high, low], axis=0)
    main = jnp.dot(both, w_high[...], preferred_element_type=F32)
    rest = jnp.dot(high, w_low[...], preferred_element_type=F32)
    return main[:F] + main[F:] + rest


def self_product(terms, fields, a):
    return sum(terms[(min(a, b), max(a, b))] * fields[b] for b in range(3))


def spread(rows):
    return [jnp.broadcast_to(r, (G, A)) for r in rows]


def own_kernel(*refs):
    inputs, outputs, buffers, arrived = refs[:8], refs[8:16], refs[16:24], refs[24]
    payload, w_high, w_low, partial, self_out, counts, state, place = outputs
    copies = [
        pltpu.make_async_copy(source, target, arrived.at[i])
        for i, (source, target) in enumerate(zip(inputs, buffers))
    ]
    for copy in copies:
        copy.start()
    entries, pos, spring, border, vec, heat, vec0, heat0 = buffers
    copies[0].wait()
    counters = count_slots(entries[...], far_groups() + [16, 17, 18, 19])
    for i in range(8):
        counts[i] = counters[i]
    for copy in copies[1:]:
        copy.wait()
    root = jnp.sqrt(spring[...])
    home = spread([pos[0], pos[1], pos[2], root])
    place[...] = jnp.concatenate([pos[0], pos[1], pos[2], root, jnp.zeros((4, A), F32)], axis=0)
    geo = place[...].T
    sums = {}
    for t in range(4):
        source = spread([geo[t * G : (t + 1) * G, c : c + 1] for c in range(4)])
        terms = pair_terms(counters[8 + t], source, home)
        put_terms(w_high, w_low, sums, [b * A + t * G for b in range(3)], terms)
    own_terms = total(sums)
    for i, key in enumerate(KEYS):
        self_out[i : i + 1, :] = own_terms[key]
    current, previous = stacked(vec, heat), stacked(vec0, heat0)
    far = apply_weights(w_high, w_low, jnp.concatenate(current, axis=1))
    begun = []
    for a in range(3):
        inner = self_product(own_terms, current, a) - far[:, a * A : (a + 1) * A] - current[a]
        begun.append(2.0 * inner - previous[a])
        partial[a] = begun[a]
        state[a] = current[a]
    geometry = jnp.concatenate(
        [pos[0], pos[1], pos[2], spring[...], jnp.zeros((F - 4, A), F32)], axis=0
    )
    picked = functools.partial(border_lanes, border)
    lists = [picked(entries[F * s : F * (s + 1), :].astype(F32)) for s in range(4)]
    payload[0] = by_group([picked(x) for x in (*current, geometry)])
    payload[1] = by_group([picked(x) for x in begun] + [lists[3]])
    payload[2] = by_group(lists[:3] + [jnp.zeros((F, A), F32)])


def moved(block, source, target):
    shift = (target - source) % 4 * G
    return pltpu.roll(block, shift, 1) if shift else block


def geometry_of(values):
    rows = [v[0:4] for v in values.values()]
    rows.append(jnp.zeros((A - 4 * len(values), A), F32))
    geo = jnp.concatenate(rows, axis=0).T[3 * G :]
    out = {}
    for j, s in enumerate(values):
        cols = [geo[:, 4 * j + c : 4 * j + c + 1] for c in range(4)]
        out[s] = spread(cols[:3] + [jnp.sqrt(cols[3])])
    return out


def shifted(cols, s):
    rise = column_edge * s[1] * upward().astype(F32)
    return [cols[0] + column_edge * s[0], cols[1] + rise, cols[2], cols[3]]


def fill_pool(rows, starts, nx, received, pool):
    def body(row):
        for j, place in enumerate(row):
            pool[j] = block_at(received, starts, place)

    for_each_row(rows, nx, body)


def side_fields(values, quad):
    return [by_group([moved(values[s], b, g) for g, s in enumerate(quad)]) for b in range(3)]


def edge_state(quad, values, geo, blocks, edge_high, edge_low):
    for j in range(len(RING)):
        edge_high[j * A + 3 * G : (j + 1) * A, :] = jnp.zeros((G, OWN), BF16)
        edge_low[j * A + 3 * G : (j + 1) * A, :] = jnp.zeros((G, OWN), BF16)
    halves = {s: split(x) for s, x in values.items()}
    fields = side_fields(values, quad)
    begun = [by_group([moved(x, b, g) for g, x in enumerate(blocks[0])]) for b in range(3)]
    lists = [
        by_group([moved(blocks[1 if k < 3 else 0][g], k, g) for g in range(4)]) for k in range(4)
    ]
    counters = count_slots(jnp.concatenate(lists, axis=0).astype(jnp.int32), far_groups())
    there = by_group([moved(values[s][0:8], 3, g) for g, s in enumerate(quad)])
    home = spread([there[0:1], there[1:2], there[2:3], jnp.sqrt(there[3:4])])
    sums = {}
    for j, s in enumerate(RING):
        around = [(t[0] + s[0], t[1] + s[1]) for t in quad]
        source = [by_group([geo[t][c] for t in around]) for c in range(4)]
        terms = pair_terms(counters[j], shifted(source, s), home)
        put_terms(edge_high, edge_low, sums, [j * A + b * G for b in range(3)], terms)
    terms = total(sums)
    lhs = [
        jnp.concatenate(
            [
                jnp.concatenate([halves[(t[0] + s[0], t[1] + s[1])][h] for s in RING], axis=1)
                for t in quad
            ],
            axis=0,
        )
        for h in range(2)
    ]
    main = jnp.dot(jnp.concatenate(lhs, axis=0), edge_high[...], preferred_element_type=F32)
    small = jnp.dot(lhs[0], edge_low[...], preferred_element_type=F32)
    result = []
    for a in range(3):
        cut = slice(a * A, (a + 1) * A)
        sums_of = [
            main[g * F : (g + 1) * F, cut]
            + main[(4 + g) * F : (5 + g) * F, cut]
            + small[g * F : (g + 1) * F, cut]
            for g in range(4)
        ]
        inner = self_product(terms, fields, a) - by_group(sums_of)
        result.append(begun[a] + 2.0 * inner)
    return result


def pool_blocks(pool, wide):
    values = {s: pool[j] for j, s in enumerate(wide)}
    blocks = [[pool[len(wide) + 4 * k + g] for g in range(4)] for k in range(2)]
    return values, blocks


def woven(first, second):
    return jnp.concatenate([x for b in range(3) for x in (first[b], second[b])], axis=1)


def next_kernel(rows, starts, nx, n_in, place, state, partial, self_in, counts,
                own_high, own_low, *rest):
    v2, h2, begun, early, far_high, far_low, pool, edge_high, edge_low = rest[n_in:]
    fill_pool(rows, starts, nx, rest[:n_in], pool)
    values, blocks = pool_blocks(pool, KNOWN)
    geo = geometry_of(values)
    home = spread([place[c : c + 1, :] for c in range(4)])
    sums = {}
    for j, s in enumerate(RING):
        terms = pair_terms(counts[j], shifted(geo[s], s), home)
        put_terms(far_high, far_low, sums, [b * 2 * A + j * G for b in range(3)], terms)
    far_terms = total(sums)
    current = [state[b] for b in range(3)]
    sides = woven(side_fields(values, EARLY), side_fields(values, LATE))
    far = apply_weights(far_high, far_low, sides)
    second = []
    for a in range(3):
        inner = self_product(far_terms, current, a) - far[:, a * A : (a + 1) * A]
        second.append(partial[a] + 2.0 * inner)
        v2[a] = second[a][:8]
        h2[a] = second[a][8:]
    all_terms = {key: far_terms[key] + self_in[i : i + 1, :] for i, key in enumerate(KEYS)}
    far = apply_weights(own_high, own_low, jnp.concatenate(second, axis=1))
    for a in range(3):
        inner = self_product(all_terms, second, a) - far[:, a * A : (a + 1) * A] - second[a]
        begun[a] = 2.0 * inner - current[a]
    edges = edge_state(EARLY, values, geo, blocks, edge_high, edge_low)
    for a in range(3):
        early[a] = edges[a]


def last_kernel(rows, starts, nx, n_in, third, early, far_high, far_low, *rest):
    v3, h3, pool, edge_high, edge_low = rest[n_in:]
    fill_pool(rows, starts, nx, rest[:n_in], pool)
    values, blocks = pool_blocks(pool, WIDE)
    late = edge_state(LATE, values, geometry_of(values), blocks, edge_high, edge_low)
    far = apply_weights(far_high, far_low, woven([early[b] for b in range(3)], late))
    for a in range(3):
        result = third[a] - 2.0 * far[:, a * A : (a + 1) * A]
        v3[a] = result[:8]
        h3[a] = result[8:]


def call(kernel, name, out_shape, args, scratch=(), space=pltpu.VMEM):
    size = sum(x.size * x.dtype.itemsize for x in (*args, *out_shape))
    return pl.pallas_call(
        kernel,
        out_shape=out_shape,
        in_specs=[pl.BlockSpec(memory_space=space)] * len(args),
        scratch_shapes=scratch,
        name=name,
        cost_estimate=pl.CostEstimate(flops=2**20, bytes_accessed=size, transcendentals=0),
        compiler_params=pltpu.CompilerParams(vmem_limit_bytes=24 * 2**20),
    )(*args)


def shards(positions, spring, border, neighbours, vec_prev, vec_now, heat_prev, heat_now):
    nx, ny = lax.axis_size("gx"), lax.axis_size("gy")
    steps, sizes, starts, send_rows, next_rows, last_rows, links = make_plan(nx, ny)
    shape = jax.ShapeDtypeStruct
    vector = shape((3, 8, A), F32)
    pos = positions.reshape(3, 1, A)
    stiff = spring.reshape(1, A)
    entries = neighbours.reshape(NB, A)
    v0, v1, h0, h1 = (x.reshape(3, 8, A) for x in (vec_prev, vec_now, heat_prev, heat_now))
    first = [
        pltpu.with_memory_space_constraint(x, pltpu.HBM)
        for x in (entries, pos, stiff, border.reshape(1, G), v1, h1, v0, h0)
    ]
    payload, own_high, own_low, partial, self_terms, counts, state, place = call(
        own_kernel,
        "own_kernel",
        (
            shape((KINDS, F, A), F32),
            shape((OWN, OWN), BF16),
            shape((OWN, OWN), BF16),
            shape((3, F, A), F32),
            shape((6, A), F32),
            shape((8, 8, A), jnp.int32),
            shape((3, F, A), F32),
            shape((8, A), F32),
        ),
        first,
        [pltpu.VMEM(x.shape, x.dtype) for x in first] + [pltpu.SemaphoreType.DMA((8,))],
        pltpu.HBM,
    )
    received = [payload]
    for i in range(len(steps)):
        if send_rows[i][0] == tuple(range(KINDS)) and len(set(send_rows[i].values())) == 1:
            outgoing = payload
        else:
            (outgoing,) = call(
                functools.partial(relay_kernel, send_rows[i], starts, nx),
                f"relay_{i}",
                (shape((sizes[i], F, A), F32),),
                received,
            )
        received.append(lax.ppermute(outgoing, ("gx", "gy"), links[i]))
    edge = [pltpu.VMEM((8 * A, OWN), BF16)] * 2
    before = received[:-1]
    v2, h2, third, early, far_high, far_low = call(
        functools.partial(next_kernel, next_rows, starts, nx, len(before)),
        "next_kernel",
        (
            vector,
            vector,
            shape((3, F, A), F32),
            shape((3, F, A), F32),
            shape((6 * A, OWN), BF16),
            shape((6 * A, OWN), BF16),
        ),
        (place, state, partial, self_terms, counts, own_high, own_low, *before),
        [pltpu.VMEM((len(KNOWN) + 8, F, A), F32)] + edge,
    )
    v3, h3 = call(
        functools.partial(last_kernel, last_rows, starts, nx, len(received)),
        "last_kernel",
        (vector, vector),
        (third, early, far_high, far_low, *received),
        [pltpu.VMEM((len(WIDE) + 8, F, A), F32)] + edge,
    )
    whole = vec_prev.shape
    return v2.reshape(whole), v3.reshape(whole), h2.reshape(whole), h3.reshape(whole)


def solution(mesh):
    wide = P(None, None, "gx", "gy", None)
    return jax.shard_map(
        shards,
        mesh=mesh,
        in_specs=(
            P(None, "gx", "gy", None),
            P("gx", "gy", None),
            P("gx", "gy", None),
            P("gx", "gy", None, None),
            wide, wide, wide, wide,
        ),
        out_specs=(wide, wide, wide, wide),
        check_vma=False,
    )
```

```python
import functools

import jax
import jax.numpy as jnp
from jax import lax
from jax.experimental import pallas as pl
from jax.experimental.pallas import tpu as pltpu
from jax.sharding import PartitionSpec as P

column_edge = 20.0
reach_sq = 64.0
A = 128
G = 32
NB = 64
F = 16
OWN = 3 * A
F32 = jnp.float32
BF16 = jnp.bfloat16
KEYS = ((0, 0), (0, 1), (0, 2), (1, 1), (1, 2), (2, 2))
EARLY = ((-1, -1), (0, -1), (-1, 0), (1, 0))
LATE = ((1, -1), (-1, 1), (0, 1), (1, 1))
RING = EARLY + LATE
WIDE = tuple((x, y) for x in range(-2, 3) for y in range(-2, 3))
KNOWN = tuple(s for s in WIDE if s[1] < 2)
KINDS = 3


def other(i, count):
    return (i + 1) % count if i % 2 else (i - 1) % count


def routes(nx, ny):
    def pair_x(x, y):
        return x ^ 1, y

    def pair_y(x, y):
        return x, y ^ 1

    def across(x, y):
        if x in (0, nx - 1):
            return other(x, nx), y
        return x, other(y, ny)

    def beside(x, y):
        if x not in (0, nx - 1):
            return other(x, nx), y
        return (x if y % 4 in (1, 2) else other(x, nx)), other(y, ny)

    return pair_x, pair_y, across, beside, pair_x, pair_y


def class_of(x, y, nx):
    ends = {0: 0, 1: 1, nx - 2: 4, nx - 1: 5}
    return 4 * ends.get(x, 2 + x % 2) + y % 4


@functools.lru_cache(None)
def make_plan(nx, ny):
    devices = [(x, y) for x in range(nx) for y in range(ny)]
    steps = routes(nx, ny)
    source = [{f(*d): d for d in devices} for f in steps]
    known, brought = {d: {d} for d in devices}, []
    for i in range(len(steps)):
        brought.append({d: known[source[i][d]] for d in devices})
        known = {d: known[d] | brought[i][d] for d in devices}

    def at(kind, d, steps_to):
        up = 1 - d[1] % 2 * 2
        return [(kind, (d[0] + a) % nx, (d[1] + up * b) % ny) for a, b in steps_to]

    def wanted(d, wide, quad):
        return at(0, d, wide) + at(1, d, quad) + at(2, d, quad)

    soon = {d: at(1, d, EARLY) + at(2, d, EARLY) for d in devices}

    def route_of(item, d, before):
        found = [i for i in range(before) if item[1:] in brought[i][d]]
        if item in soon[d]:
            found = [i for i in found if i < len(steps) - 1]
        late = item[0] and item[1] != d[0] and (item[2] != d[1] or item[1] == d[0] ^ 1)
        return found[-1 if late else 0]

    sent = [{d: set() for d in devices} for _ in steps]

    def ask(items, d, before):
        for item in items:
            if item[1:] != d:
                i = route_of(item, d, before)
                sent[i][d].add(item)

    for d in devices:
        ask(wanted(d, WIDE, RING), d, len(steps))
    for i in reversed(range(len(steps))):
        for d in devices:
            ask(sent[i][d], source[i][d], i)

    def order(d):
        near = lambda v, count: (v + count // 2) % count
        return lambda m: (m[0], near(m[1] - d[0], nx), near(m[2] - d[1], ny))

    lists = [{d: sorted(s[d], key=order(d)) for d in devices} for s in sent]
    sizes = [max(1, *map(len, s.values())) for s in lists]
    starts = [KINDS + sum(sizes[:i]) for i in range(len(sizes))]

    def place(item, d, before):
        if item[1:] == d:
            return item[0]
        i = route_of(item, d, before)
        return starts[i] + lists[i][d].index(item)

    send_rows = [{} for _ in steps]
    last_rows, next_rows = {}, {}
    for d in devices:
        c = class_of(*d, nx)
        for i, f in enumerate(steps):
            row = tuple(place(item, d, i) for item in lists[i][f(*d)])
            assert send_rows[i].setdefault(c, row) == row
        row = tuple(place(item, d, len(steps)) for item in wanted(d, WIDE, LATE))
        assert last_rows.setdefault(c, row) == row
        row = tuple(place(item, d, len(steps)) for item in wanted(d, KNOWN, EARLY))
        assert max(row) < starts[-1] and next_rows.setdefault(c, row) == row
    links = [[(x * ny + y, f(x, y)[0] * ny + f(x, y)[1]) for x, y in devices] for f in steps]
    return steps, sizes, starts, send_rows, next_rows, last_rows, links


def for_each_row(rows, nx, body):
    x, y = lax.axis_index("gx"), lax.axis_index("gy")
    column = jnp.where(x < 2, x, jnp.where(x < nx - 2, 2 + lax.rem(x, 2), x + 6 - nx))
    mine = 4 * column + lax.rem(y, 4)
    classes = {}
    for c, row in rows.items():
        classes.setdefault(row, []).append(c)
    for row, members in classes.items():
        hit = mine == members[0]
        for c in members[1:]:
            hit = hit | (mine == c)
        pl.when(hit)(functools.partial(body, row))


def block_at(refs, starts, place):
    if place < KINDS:
        return refs[min(place, 1)][max(place - 1, 0)]
    i = max(j for j in range(len(starts)) if starts[j] <= place)
    return refs[i + 2][place - starts[i]]


def relay_kernel(rows, starts, nx, *refs):
    out = refs[-1]

    def body(row):
        for j, place in enumerate(row):
            out[j] = block_at(refs, starts, place)
        for j in range(len(row), out.shape[0]):
            out[j] = jnp.zeros((F, A), F32)

    for_each_row(rows, nx, body)


def split(x):
    high = x.astype(BF16)
    return high, (x - high.astype(F32)).astype(BF16)


def border_lanes(border, values):
    index = jnp.concatenate([border[...]] * (A // G), axis=1)
    return jnp.take_along_axis(values, jnp.broadcast_to(index, values.shape), axis=1)


def by_group(parts):
    group = lax.broadcasted_iota(jnp.int32, parts[0].shape, 1) // G
    out = parts[3]
    for q in range(3):
        out = jnp.where(group == q, parts[q], out)
    return out


def stacked(vec, heat):
    return [jnp.concatenate([vec[b], heat[b]], axis=0) for b in range(3)]


def count_slots(entries, groups):
    sub = lax.broadcasted_iota(jnp.int32, (8, A), 0)
    counters = [jnp.zeros((8, A), jnp.int32) for _ in groups]
    for n in range(NB):
        e = jnp.broadcast_to(entries[n : n + 1, :], (8, A))
        mark = jnp.where(sub == (e & 7), jnp.left_shift(jnp.int32(1), e & 24), 0)
        which = lax.shift_right_arithmetic(e, 5)
        for i, g in enumerate(groups):
            counters[i] += jnp.where(which == g, mark, 0)
    return counters


def upward():
    return 1 - 2 * lax.rem(lax.axis_index("gy"), 2)


def far_groups():
    up = upward()
    return [4 * (3 * (x + 1) + up * y + 1) for x, y in RING]


def pair_terms(counter, source, home):
    tiles = [lax.shift_right_logical(counter, 8 * q) & 255 for q in range(4)]
    count = jnp.concatenate(tiles, axis=0).astype(F32)
    d = [source[a] - home[a] for a in range(3)]
    r2 = d[0] * d[0] + d[1] * d[1] + d[2] * d[2]
    near = r2 + 1.0
    inverse = (count * (home[3] * source[3])) / ((reach_sq + r2) * near)
    c = inverse * near * (reach_sq / NB)
    bend = inverse * (2.0 * reach_sq / NB)
    g = [bend * d[a] for a in range(3)]
    return {(a, b): (g[a] * d[b] + c if a == b else g[a] * d[b]) for a, b in KEYS}


def put_terms(w_high, w_low, sums, rows, terms):
    for (a, b), value in terms.items():
        part = value[0:8] + value[8:16] + value[16:24] + value[24:32]
        sums[(a, b)] = sums[(a, b)] + part if (a, b) in sums else part
        high, low = split(value)
        for p, q in sorted({(a, b), (b, a)}):
            w_high[rows[q] : rows[q] + G, p * A : (p + 1) * A] = high
            w_low[rows[q] : rows[q] + G, p * A : (p + 1) * A] = low


def total(sums):
    return {key: jnp.sum(value, axis=0, keepdims=True) for key, value in sums.items()}


def apply_weights(w_high, w_low, lhs):
    high, low = split(jnp.concatenate(lhs, axis=1))
    both = jnp.concatenate([high, low], axis=0)
    main = jnp.dot(both, w_high, preferred_element_type=F32)
    rest = jnp.dot(high, w_low, preferred_element_type=F32)
    return main[:F] + main[F:] + rest


def self_product(terms, fields, a):
    return sum(terms[(min(a, b), max(a, b))] * fields[b] for b in range(3))


def spread(rows):
    return [jnp.broadcast_to(r, (G, A)) for r in rows]


def pack_kernel(*refs):
    inputs, payload, buffers, arrived = refs[:8], refs[8], refs[9:17], refs[17]
    copies = [
        pltpu.make_async_copy(source, target, arrived.at[i])
        for i, (source, target) in enumerate(zip(inputs, buffers))
    ]
    for copy in copies:
        copy.start()
    for copy in copies[:5]:
        copy.wait()
    pos, spring, border, vec, heat = buffers[:5]
    geometry = jnp.concatenate(
        [pos[0], pos[1], pos[2], spring[...], jnp.zeros((F - 4, A), F32)], axis=0
    )
    payload[0] = by_group([border_lanes(border, x) for x in (*stacked(vec, heat), geometry)])
    for copy in copies[5:]:
        copy.wait()


def own_kernel(pos, spring, border, vec, heat, entries, vec0, heat0,
               payload, w_high, w_low, partial, self_out, counts, state, place):
    counters = count_slots(entries[...], far_groups() + [16, 17, 18, 19])
    for i in range(8):
        counts[i] = counters[i]
    root = jnp.sqrt(spring[...])
    home = spread([pos[0], pos[1], pos[2], root])
    place[...] = jnp.concatenate([pos[0], pos[1], pos[2], root, jnp.zeros((4, A), F32)], axis=0)
    geo = place[...].T
    sums = {}
    for t in range(4):
        source = spread([geo[t * G : (t + 1) * G, c : c + 1] for c in range(4)])
        terms = pair_terms(counters[8 + t], source, home)
        put_terms(w_high, w_low, sums, [b * A + t * G for b in range(3)], terms)
    own_terms = total(sums)
    for i, key in enumerate(KEYS):
        self_out[i : i + 1, :] = own_terms[key]
    current, previous = stacked(vec, heat), stacked(vec0, heat0)
    far = apply_weights(w_high[...], w_low[...], current)
    begun = []
    for a in range(3):
        inner = self_product(own_terms, current, a) - far[:, a * A : (a + 1) * A] - current[a]
        begun.append(2.0 * inner - previous[a])
        partial[a] = begun[a]
        state[a] = current[a]
    picked = functools.partial(border_lanes, border)
    lists = [picked(entries[F * s : F * (s + 1), :].astype(F32)) for s in range(4)]
    payload[0] = by_group([picked(x) for x in begun] + [lists[3]])
    payload[1] = by_group(lists[:3] + [jnp.zeros((F, A), F32)])


def moved(block, source, target):
    shift = (target - source) % 4 * G
    return pltpu.roll(block, shift, 1) if shift else block


def geometry_of(values):
    rows = [v[0:4] for v in values.values()]
    rows.append(jnp.zeros((A - 4 * len(values), A), F32))
    geo = jnp.concatenate(rows, axis=0).T[3 * G :]
    out = {}
    for j, s in enumerate(values):
        cols = [geo[:, 4 * j + c : 4 * j + c + 1] for c in range(4)]
        out[s] = spread(cols[:3] + [jnp.sqrt(cols[3])])
    return out


def shifted(cols, s):
    rise = column_edge * s[1] * upward().astype(F32)
    return [cols[0] + column_edge * s[0], cols[1] + rise, cols[2], cols[3]]


def fill_pool(rows, starts, nx, received, pool):
    def body(row):
        for j, place in enumerate(row):
            pool[j] = block_at(received, starts, place)

    for_each_row(rows, nx, body)


def side_fields(values, quad):
    return [by_group([moved(values[s], b, g) for g, s in enumerate(quad)]) for b in range(3)]


def edge_state(quad, values, geo, blocks, edge_high, edge_low):
    for j in range(len(RING)):
        edge_high[j * A + 3 * G : (j + 1) * A, :] = jnp.zeros((G, OWN), BF16)
        edge_low[j * A + 3 * G : (j + 1) * A, :] = jnp.zeros((G, OWN), BF16)
    halves = {s: split(x) for s, x in values.items()}
    fields = side_fields(values, quad)
    begun = [by_group([moved(x, b, g) for g, x in enumerate(blocks[0])]) for b in range(3)]
    lists = [
        by_group([moved(blocks[1 if k < 3 else 0][g], k, g) for g in range(4)]) for k in range(4)
    ]
    counters = count_slots(jnp.concatenate(lists, axis=0).astype(jnp.int32), far_groups())
    there = by_group([moved(values[s][0:8], 3, g) for g, s in enumerate(quad)])
    home = spread([there[0:1], there[1:2], there[2:3], jnp.sqrt(there[3:4])])
    sums = {}
    for j, s in enumerate(RING):
        around = [(t[0] + s[0], t[1] + s[1]) for t in quad]
        source = [by_group([geo[t][c] for t in around]) for c in range(4)]
        terms = pair_terms(counters[j], shifted(source, s), home)
        put_terms(edge_high, edge_low, sums, [j * A + b * G for b in range(3)], terms)
    terms = total(sums)
    lhs = [
        jnp.concatenate(
            [
                jnp.concatenate([halves[(t[0] + s[0], t[1] + s[1])][h] for s in RING], axis=1)
                for t in quad
            ],
            axis=0,
        )
        for h in range(2)
    ]
    main = jnp.dot(jnp.concatenate(lhs, axis=0), edge_high[...], preferred_element_type=F32)
    small = jnp.dot(lhs[0], edge_low[...], preferred_element_type=F32)
    result = []
    for a in range(3):
        cut = slice(a * A, (a + 1) * A)
        sums_of = [
            main[g * F : (g + 1) * F, cut]
            + main[(4 + g) * F : (5 + g) * F, cut]
            + small[g * F : (g + 1) * F, cut]
            for g in range(4)
        ]
        inner = self_product(terms, fields, a) - by_group(sums_of)
        result.append(begun[a] + 2.0 * inner)
    return result


def pool_blocks(pool, wide):
    values = {s: pool[j] for j, s in enumerate(wide)}
    blocks = [[pool[len(wide) + 4 * k + g] for g in range(4)] for k in range(2)]
    return values, blocks


def next_kernel(rows, starts, nx, n_in, place, state, partial, self_in, counts,
                own_high, own_low, *rest):
    v2, h2, begun, far_high, far_low, pool, edge_high, edge_low = rest[n_in:]
    fill_pool(rows, starts, nx, rest[:n_in], pool)
    values, blocks = pool_blocks(pool, KNOWN)
    geo = geometry_of(values)
    home = spread([place[c : c + 1, :] for c in range(4)])
    sums = {}
    for j, s in enumerate(RING):
        terms = pair_terms(counts[j], shifted(geo[s], s), home)
        put_terms(far_high, far_low, sums, [(j // 4 * 3 + b) * A + j % 4 * G for b in range(3)], terms)
    far_terms = total(sums)
    current = [state[b] for b in range(3)]
    sides = side_fields(values, EARLY) + side_fields(values, LATE)
    far = apply_weights(far_high[...], far_low[...], sides)
    second = []
    for a in range(3):
        inner = self_product(far_terms, current, a) - far[:, a * A : (a + 1) * A]
        second.append(partial[a] + 2.0 * inner)
        v2[a] = second[a][:8]
        h2[a] = second[a][8:]
    all_terms = {key: far_terms[key] + self_in[i : i + 1, :] for i, key in enumerate(KEYS)}
    far = apply_weights(own_high[...], own_low[...], second)
    early = edge_state(EARLY, values, geo, blocks, edge_high, edge_low)
    far += apply_weights(far_high[:OWN, :], far_low[:OWN, :], early)
    for a in range(3):
        inner = self_product(all_terms, second, a) - far[:, a * A : (a + 1) * A] - second[a]
        begun[a] = 2.0 * inner - current[a]


def last_kernel(rows, starts, nx, n_in, third, far_high, far_low, *rest):
    v3, h3, pool, edge_high, edge_low = rest[n_in:]
    fill_pool(rows, starts, nx, rest[:n_in], pool)
    values, blocks = pool_blocks(pool, WIDE)
    late = edge_state(LATE, values, geometry_of(values), blocks, edge_high, edge_low)
    far = apply_weights(far_high[OWN:, :], far_low[OWN:, :], late)
    for a in range(3):
        result = third[a] - 2.0 * far[:, a * A : (a + 1) * A]
        v3[a] = result[:8]
        h3[a] = result[8:]


def call(kernel, name, out_shape, args, scratch=(), space=pltpu.VMEM):
    size = sum(x.size * x.dtype.itemsize for x in (*args, *out_shape))
    return pl.pallas_call(
        kernel,
        out_shape=out_shape,
        in_specs=[pl.BlockSpec(memory_space=space)] * len(args),
        out_specs=[pl.BlockSpec(memory_space=pltpu.VMEM)] * len(out_shape),
        scratch_shapes=scratch,
        name=name,
        cost_estimate=pl.CostEstimate(flops=2**20, bytes_accessed=size, transcendentals=0),
        compiler_params=pltpu.CompilerParams(vmem_limit_bytes=24 * 2**20),
    )(*args)


def shards(positions, spring, border, neighbours, vec_prev, vec_now, heat_prev, heat_now):
    nx, ny = lax.axis_size("gx"), lax.axis_size("gy")
    steps, sizes, starts, send_rows, next_rows, last_rows, links = make_plan(nx, ny)
    shape = jax.ShapeDtypeStruct
    vector = shape((3, 8, A), F32)
    pos = positions.reshape(3, 1, A)
    stiff = spring.reshape(1, A)
    entries = neighbours.reshape(NB, A)
    v0, v1, h0, h1 = (x.reshape(3, 8, A) for x in (vec_prev, vec_now, heat_prev, heat_now))
    index = border.reshape(1, G)
    first = [
        pltpu.with_memory_space_constraint(x, pltpu.HBM)
        for x in (pos, stiff, index, v1, h1, entries, v0, h0)
    ]
    fields, *first = call(
        pack_kernel,
        "pack_kernel",
        (shape((1, F, A), F32), *(shape(x.shape, x.dtype) for x in first)),
        first,
        [pltpu.SemaphoreType.DMA((8,))],
        pltpu.HBM,
    )
    lists, own_high, own_low, partial, self_terms, counts, state, place = call(
        own_kernel,
        "own_kernel",
        (
            shape((2, F, A), F32),
            shape((OWN, OWN), BF16),
            shape((OWN, OWN), BF16),
            shape((3, F, A), F32),
            shape((6, A), F32),
            shape((8, 8, A), jnp.int32),
            shape((3, F, A), F32),
            shape((8, A), F32),
        ),
        first,
    )
    received = [fields, lists]
    for i in range(len(steps)):
        if i == 0 and set(send_rows[0].values()) == {(0,)}:
            outgoing = fields
        else:
            (outgoing,) = call(
                functools.partial(relay_kernel, send_rows[i], starts, nx),
                f"relay_{i}",
                (shape((sizes[i], F, A), F32),),
                received,
            )
        received.append(lax.ppermute(outgoing, ("gx", "gy"), links[i]))
    edge = [pltpu.VMEM((8 * A, OWN), BF16)] * 2
    before = received[:-1]
    v2, h2, third, far_high, far_low = call(
        functools.partial(next_kernel, next_rows, starts, nx, len(before)),
        "next_kernel",
        (
            vector,
            vector,
            shape((3, F, A), F32),
            shape((6 * A, OWN), BF16),
            shape((6 * A, OWN), BF16),
        ),
        (place, state, partial, self_terms, counts, own_high, own_low, *before),
        [pltpu.VMEM((len(KNOWN) + 8, F, A), F32)] + edge,
    )
    v3, h3 = call(
        functools.partial(last_kernel, last_rows, starts, nx, len(received)),
        "last_kernel",
        (vector, vector),
        (third, far_high, far_low, *received),
        [pltpu.VMEM((len(WIDE) + 8, F, A), F32)] + edge,
    )
    whole = vec_prev.shape
    return v2.reshape(whole), v3.reshape(whole), h2.reshape(whole), h3.reshape(whole)


def solution(mesh):
    wide = P(None, None, "gx", "gy", None)
    return jax.shard_map(
        shards,
        mesh=mesh,
        in_specs=(
            P(None, "gx", "gy", None),
            P("gx", "gy", None),
            P("gx", "gy", None),
            P("gx", "gy", None, None),
            wide, wide, wide, wide,
        ),
        out_specs=(wide, wide, wide, wide),
        check_vma=False,
    )
```

```python
import functools

import jax
import jax.numpy as jnp
from jax import lax
from jax.experimental import pallas as pl
from jax.experimental.pallas import tpu as pltpu
from jax.sharding import PartitionSpec as P

column_edge = 20.0
reach_sq = 64.0
A = 128
G = 32
NB = 64
F = 16
OWN = 3 * A
F32 = jnp.float32
BF16 = jnp.bfloat16
KEYS = ((0, 0), (0, 1), (0, 2), (1, 1), (1, 2), (2, 2))
EARLY = ((-1, -1), (0, -1), (-1, 0), (1, 0))
LATE = ((1, -1), (-1, 1), (0, 1), (1, 1))
RING = EARLY + LATE
WIDE = tuple((x, y) for x in range(-2, 3) for y in range(-2, 3))
KNOWN = tuple(s for s in WIDE if s[1] < 2)
KINDS = 3


def other(i, count):
    return (i + 1) % count if i % 2 else (i - 1) % count


def routes(nx, ny):
    def pair_x(x, y):
        return x ^ 1, y

    def pair_y(x, y):
        return x, y ^ 1

    def across(x, y):
        return other(x, nx), other(y, ny)

    def beside(x, y):
        if x in (0, nx - 1) and y % 4 in (1, 2):
            return x, other(y, ny)
        return other(x, nx), y

    return pair_x, pair_y, across, beside, pair_x, pair_y


def class_of(x, y, nx):
    ends = {0: 0, 1: 1, nx - 2: 4, nx - 1: 5}
    return 4 * ends.get(x, 2 + x % 2) + y % 4


@functools.lru_cache(None)
def make_plan(nx, ny):
    devices = [(x, y) for x in range(nx) for y in range(ny)]
    steps = routes(nx, ny)
    source = [{f(*d): d for d in devices} for f in steps]
    known, brought = {d: {d} for d in devices}, []
    for i in range(len(steps)):
        brought.append({d: known[source[i][d]] for d in devices})
        known = {d: known[d] | brought[i][d] for d in devices}

    def at(kind, d, steps_to):
        up = 1 - d[1] % 2 * 2
        return [(kind, (d[0] + a) % nx, (d[1] + up * b) % ny) for a, b in steps_to]

    def wanted(d, wide, quad):
        return at(0, d, wide) + at(1, d, quad) + at(2, d, quad)

    soon = {d: at(1, d, EARLY) + at(2, d, EARLY) for d in devices}

    def route_of(item, d, before):
        found = [i for i in range(before) if item[1:] in brought[i][d]]
        if item in soon[d]:
            found = [i for i in found if i < len(steps) - 1]
        late = item[0] and item[1] != d[0] and (item[2] != d[1] or item[1] == d[0] ^ 1)
        return found[-1 if late else 0]

    sent = [{d: set() for d in devices} for _ in steps]

    def ask(items, d, before):
        for item in items:
            if item[1:] != d:
                i = route_of(item, d, before)
                sent[i][d].add(item)

    for d in devices:
        ask(wanted(d, WIDE, RING), d, len(steps))
    for i in reversed(range(len(steps))):
        for d in devices:
            ask(sent[i][d], source[i][d], i)

    def order(d):
        near = lambda v, count: (v + count // 2) % count
        return lambda m: (m[0], near(m[1] - d[0], nx), near(m[2] - d[1], ny))

    lists = [{d: sorted(s[d], key=order(d)) for d in devices} for s in sent]
    sizes = [max(1, *map(len, s.values())) for s in lists]
    starts = [KINDS + sum(sizes[:i]) for i in range(len(sizes))]

    def place(item, d, before):
        if item[1:] == d:
            return item[0]
        i = route_of(item, d, before)
        return starts[i] + lists[i][d].index(item)

    send_rows = [{} for _ in steps]
    last_rows, next_rows = {}, {}
    for d in devices:
        c = class_of(*d, nx)
        for i, f in enumerate(steps):
            row = tuple(place(item, d, i) for item in lists[i][f(*d)])
            assert send_rows[i].setdefault(c, row) == row
        row = tuple(place(item, d, len(steps)) for item in wanted(d, WIDE, LATE))
        assert last_rows.setdefault(c, row) == row
        row = tuple(place(item, d, len(steps)) for item in wanted(d, KNOWN, EARLY))
        assert max(row) < starts[-1] and next_rows.setdefault(c, row) == row
    links = [[(x * ny + y, f(x, y)[0] * ny + f(x, y)[1]) for x, y in devices] for f in steps]
    return steps, sizes, starts, send_rows, next_rows, last_rows, links


def for_each_row(rows, nx, body):
    x, y = lax.axis_index("gx"), lax.axis_index("gy")
    column = jnp.where(x < 2, x, jnp.where(x < nx - 2, 2 + lax.rem(x, 2), x + 6 - nx))
    mine = 4 * column + lax.rem(y, 4)
    classes = {}
    for c, row in rows.items():
        classes.setdefault(row, []).append(c)
    for row, members in classes.items():
        hit = mine == members[0]
        for c in members[1:]:
            hit = hit | (mine == c)
        pl.when(hit)(functools.partial(body, row))


def block_at(refs, starts, place):
    if place < KINDS:
        return refs[min(place, 1)][max(place - 1, 0)]
    i = max(j for j in range(len(starts)) if starts[j] <= place)
    return refs[i + 2][place - starts[i]]


def relay_kernel(rows, starts, nx, *refs):
    out = refs[-1]

    def body(row):
        for j, place in enumerate(row):
            out[j] = block_at(refs, starts, place)
        for j in range(len(row), out.shape[0]):
            out[j] = jnp.zeros((F, A), F32)

    for_each_row(rows, nx, body)


def split(x):
    high = x.astype(BF16)
    return high, (x - high.astype(F32)).astype(BF16)


def border_lanes(border, values):
    index = jnp.concatenate([border[...]] * (A // G), axis=1)
    return jnp.take_along_axis(values, jnp.broadcast_to(index, values.shape), axis=1)


def by_group(parts):
    group = lax.broadcasted_iota(jnp.int32, parts[0].shape, 1) // G
    out = parts[3]
    for q in range(3):
        out = jnp.where(group == q, parts[q], out)
    return out


def stacked(vec, heat):
    return [jnp.concatenate([vec[b], heat[b]], axis=0) for b in range(3)]


def count_slots(entries, groups):
    sub = lax.broadcasted_iota(jnp.int32, (8, A), 0)
    counters = [jnp.zeros((8, A), jnp.int32) for _ in groups]
    for n in range(NB):
        e = jnp.broadcast_to(entries[n : n + 1, :], (8, A))
        mark = jnp.where(sub == (e & 7), jnp.left_shift(jnp.int32(1), e & 24), 0)
        which = lax.shift_right_arithmetic(e, 5)
        for i, g in enumerate(groups):
            counters[i] += jnp.where(which == g, mark, 0)
    return counters


def upward():
    return 1 - 2 * lax.rem(lax.axis_index("gy"), 2)


def far_groups():
    up = upward()
    return [4 * (3 * (x + 1) + up * y + 1) for x, y in RING]


def pair_terms(counter, source, home):
    tiles = [lax.shift_right_logical(counter, 8 * q) & 255 for q in range(4)]
    count = jnp.concatenate(tiles, axis=0).astype(F32)
    d = [source[a] - home[a] for a in range(3)]
    r2 = d[0] * d[0] + d[1] * d[1] + d[2] * d[2]
    near = r2 + 1.0
    inverse = (count * (home[3] * source[3])) / ((reach_sq + r2) * near)
    c = inverse * near * (reach_sq / NB)
    bend = inverse * (2.0 * reach_sq / NB)
    g = [bend * d[a] for a in range(3)]
    return {(a, b): (g[a] * d[b] + c if a == b else g[a] * d[b]) for a, b in KEYS}


def put_terms(w_high, w_low, sums, rows, terms):
    for (a, b), value in terms.items():
        part = value[0:8] + value[8:16] + value[16:24] + value[24:32]
        sums[(a, b)] = sums[(a, b)] + part if (a, b) in sums else part
        high, low = split(value)
        for p, q in sorted({(a, b), (b, a)}):
            w_high[rows[q] : rows[q] + G, p * A : (p + 1) * A] = high
            w_low[rows[q] : rows[q] + G, p * A : (p + 1) * A] = low


def total(sums):
    return {key: jnp.sum(value, axis=0, keepdims=True) for key, value in sums.items()}


def apply_weights(w_high, w_low, lhs):
    high, low = split(jnp.concatenate(lhs, axis=1))
    both = jnp.concatenate([high, low], axis=0)
    main = jnp.dot(both, w_high, preferred_element_type=F32)
    rest = jnp.dot(high, w_low, preferred_element_type=F32)
    return main[:F] + main[F:] + rest


def self_product(terms, fields, a):
    return sum(terms[(min(a, b), max(a, b))] * fields[b] for b in range(3))


def spread(rows):
    return [jnp.broadcast_to(r, (G, A)) for r in rows]


def pack_kernel(*refs):
    inputs, payload, buffers, arrived = refs[:8], refs[8], refs[9:17], refs[17]
    copies = [
        pltpu.make_async_copy(source, target, arrived.at[i])
        for i, (source, target) in enumerate(zip(inputs, buffers))
    ]
    for copy in copies:
        copy.start()
    for copy in copies[:5]:
        copy.wait()
    pos, spring, border, vec, heat = buffers[:5]
    geometry = jnp.concatenate(
        [pos[0], pos[1], pos[2], spring[...], jnp.zeros((F - 4, A), F32)], axis=0
    )
    payload[0] = by_group([border_lanes(border, x) for x in (*stacked(vec, heat), geometry)])
    for copy in copies[5:]:
        copy.wait()


def own_kernel(pos, spring, border, vec, heat, entries, vec0, heat0,
               payload, w_high, w_low, partial, self_out, counts, state, place):
    counters = count_slots(entries[...], far_groups() + [16, 17, 18, 19])
    for i in range(8):
        counts[i] = counters[i]
    root = jnp.sqrt(spring[...])
    home = spread([pos[0], pos[1], pos[2], root])
    place[...] = jnp.concatenate([pos[0], pos[1], pos[2], root, jnp.zeros((4, A), F32)], axis=0)
    geo = place[...].T
    sums = {}
    for t in range(4):
        source = spread([geo[t * G : (t + 1) * G, c : c + 1] for c in range(4)])
        terms = pair_terms(counters[8 + t], source, home)
        put_terms(w_high, w_low, sums, [b * A + t * G for b in range(3)], terms)
    own_terms = total(sums)
    for i, key in enumerate(KEYS):
        self_out[i : i + 1, :] = own_terms[key]
    current, previous = stacked(vec, heat), stacked(vec0, heat0)
    far = apply_weights(w_high[...], w_low[...], current)
    begun = []
    for a in range(3):
        inner = self_product(own_terms, current, a) - far[:, a * A : (a + 1) * A] - current[a]
        begun.append(2.0 * inner - previous[a])
        partial[a] = begun[a]
        state[a] = current[a]
    picked = functools.partial(border_lanes, border)
    lists = [picked(entries[F * s : F * (s + 1), :].astype(F32)) for s in range(4)]
    payload[0] = by_group([picked(x) for x in begun] + [lists[3]])
    payload[1] = by_group(lists[:3] + [jnp.zeros((F, A), F32)])


def moved(block, source, target):
    shift = (target - source) % 4 * G
    return pltpu.roll(block, shift, 1) if shift else block


def geometry_of(values):
    rows = [v[0:4] for v in values.values()]
    rows.append(jnp.zeros((A - 4 * len(values), A), F32))
    geo = jnp.concatenate(rows, axis=0).T[3 * G :]
    out = {}
    for j, s in enumerate(values):
        cols = [geo[:, 4 * j + c : 4 * j + c + 1] for c in range(4)]
        out[s] = spread(cols[:3] + [jnp.sqrt(cols[3])])
    return out


def shifted(cols, s):
    rise = column_edge * s[1] * upward().astype(F32)
    return [cols[0] + column_edge * s[0], cols[1] + rise, cols[2], cols[3]]


def fill_pool(rows, starts, nx, received, pool):
    def body(row):
        for j, place in enumerate(row):
            pool[j] = block_at(received, starts, place)

    for_each_row(rows, nx, body)


def side_fields(values, quad):
    return [by_group([moved(values[s], b, g) for g, s in enumerate(quad)]) for b in range(3)]


def edge_state(quad, values, geo, blocks, edge_high, edge_low):
    for j in range(len(RING)):
        edge_high[j * A + 3 * G : (j + 1) * A, :] = jnp.zeros((G, OWN), BF16)
        edge_low[j * A + 3 * G : (j + 1) * A, :] = jnp.zeros((G, OWN), BF16)
    halves = {s: split(x) for s, x in values.items()}
    fields = side_fields(values, quad)
    begun = [by_group([moved(x, b, g) for g, x in enumerate(blocks[0])]) for b in range(3)]
    lists = [
        by_group([moved(blocks[1 if k < 3 else 0][g], k, g) for g in range(4)]) for k in range(4)
    ]
    counters = count_slots(jnp.concatenate(lists, axis=0).astype(jnp.int32), far_groups())
    there = by_group([moved(values[s][0:8], 3, g) for g, s in enumerate(quad)])
    home = spread([there[0:1], there[1:2], there[2:3], jnp.sqrt(there[3:4])])
    sums = {}
    for j, s in enumerate(RING):
        around = [(t[0] + s[0], t[1] + s[1]) for t in quad]
        source = [by_group([geo[t][c] for t in around]) for c in range(4)]
        terms = pair_terms(counters[j], shifted(source, s), home)
        put_terms(edge_high, edge_low, sums, [j * A + b * G for b in range(3)], terms)
    terms = total(sums)
    lhs = [
        jnp.concatenate(
            [
                jnp.concatenate([halves[(t[0] + s[0], t[1] + s[1])][h] for s in RING], axis=1)
                for t in quad
            ],
            axis=0,
        )
        for h in range(2)
    ]
    main = jnp.dot(jnp.concatenate(lhs, axis=0), edge_high[...], preferred_element_type=F32)
    small = jnp.dot(lhs[0], edge_low[...], preferred_element_type=F32)
    result = []
    for a in range(3):
        cut = slice(a * A, (a + 1) * A)
        sums_of = [
            main[g * F : (g + 1) * F, cut]
            + main[(4 + g) * F : (5 + g) * F, cut]
            + small[g * F : (g + 1) * F, cut]
            for g in range(4)
        ]
        inner = self_product(terms, fields, a) - by_group(sums_of)
        result.append(begun[a] + 2.0 * inner)
    return result


def pool_blocks(pool, wide):
    values = {s: pool[j] for j, s in enumerate(wide)}
    blocks = [[pool[len(wide) + 4 * k + g] for g in range(4)] for k in range(2)]
    return values, blocks


def next_kernel(rows, starts, nx, n_in, place, state, partial, self_in, counts,
                own_high, own_low, *rest):
    v2, h2, begun, far_high, far_low, pool, edge_high, edge_low = rest[n_in:]
    fill_pool(rows, starts, nx, rest[:n_in], pool)
    values, blocks = pool_blocks(pool, KNOWN)
    geo = geometry_of(values)
    home = spread([place[c : c + 1, :] for c in range(4)])
    sums = {}
    for j, s in enumerate(RING):
        terms = pair_terms(counts[j], shifted(geo[s], s), home)
        put_terms(far_high, far_low, sums, [(j // 4 * 3 + b) * A + j % 4 * G for b in range(3)], terms)
    far_terms = total(sums)
    current = [state[b] for b in range(3)]
    sides = side_fields(values, EARLY) + side_fields(values, LATE)
    far = apply_weights(far_high[...], far_low[...], sides)
    second = []
    for a in range(3):
        inner = self_product(far_terms, current, a) - far[:, a * A : (a + 1) * A]
        second.append(partial[a] + 2.0 * inner)
        v2[a] = second[a][:8]
        h2[a] = second[a][8:]
    all_terms = {key: far_terms[key] + self_in[i : i + 1, :] for i, key in enumerate(KEYS)}
    far = apply_weights(own_high[...], own_low[...], second)
    early = edge_state(EARLY, values, geo, blocks, edge_high, edge_low)
    far += apply_weights(far_high[:OWN, :], far_low[:OWN, :], early)
    for a in range(3):
        inner = self_product(all_terms, second, a) - far[:, a * A : (a + 1) * A] - second[a]
        begun[a] = 2.0 * inner - current[a]


def last_kernel(rows, starts, nx, n_in, third, far_high, far_low, *rest):
    v3, h3, pool, edge_high, edge_low = rest[n_in:]
    fill_pool(rows, starts, nx, rest[:n_in], pool)
    values, blocks = pool_blocks(pool, WIDE)
    late = edge_state(LATE, values, geometry_of(values), blocks, edge_high, edge_low)
    far = apply_weights(far_high[OWN:, :], far_low[OWN:, :], late)
    for a in range(3):
        result = third[a] - 2.0 * far[:, a * A : (a + 1) * A]
        v3[a] = result[:8]
        h3[a] = result[8:]


def call(kernel, name, out_shape, args, scratch=(), space=pltpu.VMEM):
    size = sum(x.size * x.dtype.itemsize for x in (*args, *out_shape))
    return pl.pallas_call(
        kernel,
        out_shape=out_shape,
        in_specs=[pl.BlockSpec(memory_space=space)] * len(args),
        out_specs=[pl.BlockSpec(memory_space=pltpu.VMEM)] * len(out_shape),
        scratch_shapes=scratch,
        name=name,
        cost_estimate=pl.CostEstimate(flops=2**20, bytes_accessed=size, transcendentals=0),
        compiler_params=pltpu.CompilerParams(vmem_limit_bytes=24 * 2**20),
    )(*args)


def shards(positions, spring, border, neighbours, vec_prev, vec_now, heat_prev, heat_now):
    nx, ny = lax.axis_size("gx"), lax.axis_size("gy")
    steps, sizes, starts, send_rows, next_rows, last_rows, links = make_plan(nx, ny)
    shape = jax.ShapeDtypeStruct
    vector = shape((3, 8, A), F32)
    pos = positions.reshape(3, 1, A)
    stiff = spring.reshape(1, A)
    entries = neighbours.reshape(NB, A)
    v0, v1, h0, h1 = (x.reshape(3, 8, A) for x in (vec_prev, vec_now, heat_prev, heat_now))
    index = border.reshape(1, G)
    first = [
        pltpu.with_memory_space_constraint(x, pltpu.HBM)
        for x in (pos, stiff, index, v1, h1, entries, v0, h0)
    ]
    fields, *first = call(
        pack_kernel,
        "pack_kernel",
        (shape((1, F, A), F32), *(shape(x.shape, x.dtype) for x in first)),
        first,
        [pltpu.SemaphoreType.DMA((8,))],
        pltpu.HBM,
    )
    lists, own_high, own_low, partial, self_terms, counts, state, place = call(
        own_kernel,
        "own_kernel",
        (
            shape((2, F, A), F32),
            shape((OWN, OWN), BF16),
            shape((OWN, OWN), BF16),
            shape((3, F, A), F32),
            shape((6, A), F32),
            shape((8, 8, A), jnp.int32),
            shape((3, F, A), F32),
            shape((8, A), F32),
        ),
        first,
    )
    received = [fields, lists]
    for i in range(len(steps)):
        if i == 0 and set(send_rows[0].values()) == {(0,)}:
            outgoing = fields
        else:
            (outgoing,) = call(
                functools.partial(relay_kernel, send_rows[i], starts, nx),
                f"relay_{i}",
                (shape((sizes[i], F, A), F32),),
                received,
            )
        received.append(lax.ppermute(outgoing, ("gx", "gy"), links[i]))
    edge = [pltpu.VMEM((8 * A, OWN), BF16)] * 2
    before = received[:-1]
    v2, h2, third, far_high, far_low = call(
        functools.partial(next_kernel, next_rows, starts, nx, len(before)),
        "next_kernel",
        (
            vector,
            vector,
            shape((3, F, A), F32),
            shape((6 * A, OWN), BF16),
            shape((6 * A, OWN), BF16),
        ),
        (place, state, partial, self_terms, counts, own_high, own_low, *before),
        [pltpu.VMEM((len(KNOWN) + 8, F, A), F32)] + edge,
    )
    v3, h3 = call(
        functools.partial(last_kernel, last_rows, starts, nx, len(received)),
        "last_kernel",
        (vector, vector),
        (third, far_high, far_low, *received),
        [pltpu.VMEM((len(WIDE) + 8, F, A), F32)] + edge,
    )
    whole = vec_prev.shape
    return v2.reshape(whole), v3.reshape(whole), h2.reshape(whole), h3.reshape(whole)


def solution(mesh):
    wide = P(None, None, "gx", "gy", None)
    return jax.shard_map(
        shards,
        mesh=mesh,
        in_specs=(
            P(None, "gx", "gy", None),
            P("gx", "gy", None),
            P("gx", "gy", None),
            P("gx", "gy", None, None),
            wide, wide, wide, wide,
        ),
        out_specs=(wide, wide, wide, wide),
        check_vma=False,
    )
```
